512 devices in a mesh: band: 32 (over z_hi, y, x), pair: 16 (over z_lo, core).
Axes of the slice: x: 4, y: 4, z: 16 (z_hi: 2, z_lo: 8; z = z_hi * 8 + z_lo), core: 2. Of those that a mesh axis runs over, the one named last changes fastest.
Arguments:
- orbitals: bfloat16 [64, 32, 1024], P('band'), may hold values from -6 to 6
- kernel: float32 [32, 1024], replicated, may hold values from 0 to 1.2, as said below
- occupations: float32 [64], replicated, may hold values from 0.04 to 0.99
- plan: int32 [32], replicated, may hold values from 0 to 31, each once
Outputs:
- exchange: float32 [64, 32, 1024], P('band', 'pair')
- slot_energy: float32 [32], P('pair')
The draws below stay inside these ranges and needn't reach their ends.
Inputs may be any that keep to these rules, and one draw needn't show every extreme that they name: `plan`: each owner distance 0 to 31 appears exactly once. kernel is unchanged when any one frequency index i is replaced by (32 - i) % 32, and is not negative.
All inputs are finite; a program needn't handle non-finite values.
Results may differ from the reference program's by a relative error of at most 0.0004.
Values may be sent and summed in bfloat16 or wider, within the bound.
No kernel may reach another device: no remote copies, remote signals or barrier semaphores. Data moves between devices by JAX's collectives and lax.ppermute only.
A program may use at most 64 MiB of HBM per device.

```python
import math
import jax
import jax.numpy as jnp
from jax import lax

L = 32
ORB_DEV = 2
ORBITALS = 64
N_BAND = 32


def draw_kernel(key, part):
    half = L // 2
    key_radius, key_rough = jax.random.split(jax.random.fold_in(key, 11))
    radius = jax.random.uniform(key_radius, (), jnp.float32, 1.5, 3.0)
    rough = jax.random.uniform(key_rough, (half + 1, half + 1, half + 1), jnp.float32, 0.8, 1.2)
    index = jnp.arange(L, dtype=jnp.int32)
    folded = jnp.where(index <= half, index, L - index)
    wave = folded.astype(jnp.float32) * (2.0 * math.pi / L)
    squared = wave[:, None, None] ** 2 + wave[None, :, None] ** 2 + wave[None, None, :] ** 2
    scaled = jnp.sqrt(squared) * radius
    safe = jnp.maximum(scaled, 0.001)
    base = jnp.where(scaled < 0.001, 1.0, 2.0 * (1.0 - jnp.cos(safe)) / (safe * safe))
    factor = rough[folded][:, folded][:, :, folded]
    return (base * factor).reshape(L, L * L)


def draw_occupations(key, part):
    noise = jax.random.uniform(jax.random.fold_in(key, 23), (ORBITALS,), jnp.float32, -0.3, 0.3)
    level = jnp.linspace(-2.5, 1.5, ORBITALS) + noise
    return jax.nn.sigmoid(-level)


def shard_levels(stream_key, extent, cuts, smallest, high):
    factor_of = 1.0
    for axis_at, blocks in cuts:
        steps = jax.random.uniform(jax.random.fold_in(jax.random.fold_in(stream_key, 6), axis_at), (blocks,), jnp.float32, smallest / len(cuts), high / len(cuts))
        factor_of = factor_of * jnp.repeat(jnp.exp(steps), extent[axis_at] // blocks).reshape((-1,) + (1,) * (len(extent) - 1 - axis_at))
    return factor_of


def bell_draw(own_key, extent, spread, reach, shards=(), kind=jnp.bfloat16):
    result = spread * jax.random.normal(own_key, extent, jnp.float32)
    if shards:
        result = result * shard_levels(own_key, extent, shards, -0.22, 0.18)
    return jnp.clip(result, -reach, reach).astype(kind)


def setup_inputs(seed: int = 0) -> dict:
    seeds = jax.random.split(jax.random.key(seed), 5)
    orbitals = bell_draw(seeds[0], (ORBITALS, L, L * L), 1.0, 6.0, ((0, 32),))
    kernel = draw_kernel(jax.random.fold_in(seeds[4], 71), 0)
    occupations = draw_occupations(jax.random.fold_in(seeds[4], 71), 0)
    plan = jax.random.permutation(seeds[3], N_BAND).astype(jnp.int32)
    return dict(orbitals=orbitals, kernel=kernel, occupations=occupations, plan=plan)


def reference(orbitals, kernel, occupations, plan):
    fields = orbitals.astype(jnp.float32).reshape(ORBITALS, L, L, L)
    multiplier = kernel.reshape(L, L, L)[:, :, : L // 2 + 1]
    weighted = fields * occupations[:, None, None, None]

    def one_orbital(target):
        density = fields * target[None]
        spectrum = jnp.fft.rfftn(density, axes=(1, 2, 3))
        potential = jnp.fft.irfftn(spectrum * multiplier[None], s=(L, L, L), axes=(1, 2, 3))
        applied = -jnp.sum(potential * weighted, axis=0)
        inner = jnp.sum(potential * density, axis=(1, 2, 3))
        return applied, inner

    applied, inner = lax.map(one_orbital, fields)
    pair_sum = occupations[:, None] * occupations[None, :] * inner
    owner = jnp.arange(ORBITALS, dtype=jnp.int32) // ORB_DEV
    distance = jnp.bitwise_xor(owner[:, None], owner[None, :])
    levels = jnp.arange(N_BAND, dtype=jnp.int32)
    onehot = (distance[:, :, None] == levels[None, None, :]).astype(jnp.float32)
    by_distance = jnp.sum(pair_sum[:, :, None] * onehot, axis=(0, 1))
    pick = (plan[:, None] == levels[None, :]).astype(jnp.float32)
    slot_energy = -jnp.sum(pick * by_distance[None, :], axis=1) / (2.0 * ORBITALS * L ** 3)
    return applied.reshape(ORBITALS, L, L * L), slot_energy
```

```python
import functools
import math

import jax
import jax.numpy as jnp
import ml_dtypes
import numpy as np
from jax import lax
from jax.experimental import pallas as pl
from jax.experimental.pallas import tpu as pltpu
from jax.sharding import Mesh
from jax.sharding import PartitionSpec as P

AXES = ("zh", "y", "x", "zl", "core")
BAND = ("zh", "y", "x")
PAIR = ("zl", "core")
SIZES = (2, 4, 4, 8, 2)

STEPS = (
    ((2, 2), (2, 1)),
    ((2, 3), (3, 2)),
    ((3, 3), (3, 1)),
    ((0, 0), (1, 0)),
    ((0, 1), (0, 3)),
    ((1, 3), (1, 1)),
    ((0, 2), (3, 0)),
    ((1, 2), (2, 0)),
)


def step_of(zh, zl, core):
    return STEPS[zl if zh == 0 else SIZES[3] - 1 - zl][core]


def place(coords):
    flat = 0
    for size, at in zip(SIZES, coords):
        flat = flat * size + at
    return flat


def routes(move):
    return [(place(c), place(move(*c))) for c in np.ndindex(*SIZES)]


def same_half(zh, y, x, zl, core):
    dy, dx = step_of(zh, zl, core)
    return zh, y ^ dy, x ^ dx, zl, core


def other_half(zh, y, x, zl, core):
    dy, dx = step_of(zh, zl, core)
    return 1 - zh, y ^ dy, x ^ dx, SIZES[3] - 1 - zl, core


def mirror(zh, y, x, zl, core):
    return 1 - zh, y, x, SIZES[3] - 1 - zl, core


def other_core(zh, y, x, zl, core):
    return zh, y, x, zl, 1 - core


def two_parts(matrix):
    high = matrix.astype(ml_dtypes.bfloat16)
    low = (matrix - high.astype(np.float64)).astype(ml_dtypes.bfloat16)
    return np.stack([high, low])


def hartley(points):
    at = np.arange(points)
    angle = (np.outer(at, at) % points) * (2.0 * math.pi / points)
    return (np.cos(angle) + np.sin(angle)) / math.sqrt(points)


def mode_order(points):
    at = np.arange(points)
    return np.concatenate([at[0::4], at[2::4], at[1::2]])


@functools.cache
def tables(points, own, groups, cores):
    base = hartley(points)
    quarter = base[:, : points // 4]
    quarters = np.kron(quarter[0::4].T, base)
    halves = np.kron(quarter[2::4].T, base)
    odd = np.kron(base[1::2, : points // 2].T, base)
    pairs = own * own
    along = np.kron(np.eye(pairs), base)
    planes = points // groups
    rows = []
    for core in range(cores):
        for zl in range(groups // cores):
            for a in range(own):
                for low in range(planes):
                    rows.append((a, (zl * cores + core) * planes + low))
    picks = []
    spread = np.zeros((pairs * points, own * points))
    for b in range(own):
        for a, plane in rows:
            spread[len(picks), b * points + plane] = 1.0
            picks.append((b * own + a) * points + plane)
    return dict(
        along=two_parts(along).reshape(2 * pairs * points, pairs * points),
        back=two_parts(along[picks]).reshape(2 * pairs * points, pairs * points),
        spread=spread.astype(ml_dtypes.bfloat16),
        quarters=two_parts(quarters),
        halves=two_parts(halves),
        odd=two_parts(odd),
    )


NAMES = ("along", "back", "spread", "quarters", "halves", "odd")


def split(value):
    high = value.astype(jnp.bfloat16)
    return high, (value - high.astype(jnp.float32)).astype(jnp.bfloat16)


def product(left, right, contract):
    return lax.dot_general(left, right, (contract, ((), ())), preferred_element_type=jnp.float32)


def on_rows(value, matrix, contract):
    rows = value.shape[0]
    high, low = split(value)
    both = product(jnp.concatenate([high, low], axis=0), matrix[0], ((1,), (contract,)))
    rest = product(high, matrix[1], ((1,), (contract,)))
    return both[:rows] + both[rows:] + rest


def on_planes(matrix, value):
    rows = matrix.shape[0] // 2
    high, low = split(value)
    both = product(matrix, high, ((1,), (0,)))
    rest = product(matrix[:rows], low, ((1,), (0,)))
    return both[:rows] + both[rows:] + rest


def in_mode_order(kernel, points):
    order = mode_order(points)
    width = 128
    each = width // points
    lane = lax.broadcasted_iota(jnp.int32, (points, width), 1)
    columns = []
    for column in range(points * points // width):
        taken = None
        for at in range(each):
            source = int(order[column * each + at])
            block = kernel[:, source // each * width : (source // each + 1) * width]
            shift = (at - source % each) * points % width
            if shift:
                block = pltpu.roll(block, shift, 1)
            taken = block if taken is None else jnp.where(lane >= at * points, block, taken)
        columns.append(taken)
    return jnp.concatenate(columns, axis=1)


def pair_terms(mine, partner, mine_weight, partner_weight, kernel, table):
    own, points, cells = mine.shape
    pairs = own * own
    block = cells // 4
    left = mine.astype(jnp.float32)
    right = partner.astype(jnp.float32)
    modal = in_mode_order(kernel, points)
    along, back, spread = table["along"], table["back"], table["spread"]
    parts = []
    for at in range(4):
        lanes = slice(at * block, (at + 1) * block)
        density = jnp.concatenate(
            [left[a, :, lanes] * right[b, :, lanes] for b in range(own) for a in range(own)], axis=0
        )
        parts.append(on_planes(along, density))
    even0, even1 = parts[0] + parts[2], parts[1] + parts[3]
    odd = jnp.concatenate([parts[0] - parts[2], parts[1] - parts[3]], axis=1)
    spectrum = jnp.concatenate(
        [
            on_rows(even0 + even1, table["quarters"], 0),
            on_rows(even0 - even1, table["halves"], 0),
            on_rows(odd, table["odd"], 0),
        ],
        axis=1,
    )
    energies = []
    shaped = []
    for f in range(pairs):
        rows = spectrum[f * points : (f + 1) * points]
        potential = rows * modal
        shaped.append(potential)
        terms = (rows * potential).reshape(points // 8, 8, cells // 128, 128)
        energies.append(jnp.sum(terms, axis=(0, 2)))
    energy = jnp.zeros((8, 128), jnp.float32)
    straight = jnp.zeros((8, 128), jnp.float32)
    crossed = jnp.zeros((8, 128), jnp.float32)
    for b in range(own):
        for a in range(own):
            term = energies[b * own + a] * (mine_weight[a] * partner_weight[b])
            if a == b:
                straight = straight + term
            else:
                crossed = crossed + term
    energy = straight + crossed
    shaped = jnp.concatenate(shaped, axis=0)
    quarters = on_rows(shaped[:, :block], table["quarters"], 1)
    halves = on_rows(shaped[:, block : 2 * block], table["halves"], 1)
    odd = on_rows(shaped[:, 2 * block :], table["odd"], 1)
    even0, even1 = quarters + halves, quarters - halves
    odd0, odd1 = odd[:, :block], odd[:, block:]
    fields = [even0 + odd0, even1 + odd1, even0 - odd0, even1 - odd1]
    flat = partner.reshape(own * points, cells)
    rows = own * points
    pulled = []
    for at in range(4):
        potential = on_planes(back, fields[at])
        spreads = product(spread, flat[:, at * block : (at + 1) * block], ((1,), (0,)))
        total = None
        for b in range(own):
            term = potential[b * rows : (b + 1) * rows] * spreads[b * rows : (b + 1) * rows]
            term = term * partner_weight[b]
            total = term if total is None else total + term
        pulled.append(-total)
    return jnp.concatenate(pulled, axis=1), energy


def weights_of(occupation_ref, owner, own):
    return [occupation_ref[owner * own + at] for at in range(own)]


def first_body(who_ref, occupation_ref, mine_ref, partner_ref, kernel_ref, *refs):
    table = {name: ref[...] for name, ref in zip(NAMES, refs)}
    exchange_ref, energy_ref = refs[len(NAMES) :]
    own = mine_ref.shape[0]
    exchange, energy = pair_terms(
        mine_ref[...],
        partner_ref[...],
        weights_of(occupation_ref, who_ref[0], own),
        weights_of(occupation_ref, who_ref[1], own),
        kernel_ref[...],
        table,
    )
    exchange_ref[...] = exchange
    energy_ref[...] = jnp.full(energy_ref.shape, jnp.sum(energy))


def second_body(who_ref, occupation_ref, mine_ref, partner_ref, kernel_ref, *refs):
    table = {name: ref[...] for name, ref in zip(NAMES, refs)}
    before_ref, near_ref, far_ref, keep_ref, send_ref, energy_ref = refs[len(NAMES) :]
    own = mine_ref.shape[0]
    exchange, energy = pair_terms(
        mine_ref[...],
        partner_ref[...],
        weights_of(occupation_ref, who_ref[0], own),
        weights_of(occupation_ref, who_ref[2], own),
        kernel_ref[...],
        table,
    )
    exchange = exchange + before_ref[...]
    half = exchange.shape[0] // 2
    low, high = exchange[:half], exchange[half:]
    first = who_ref[3] == 0
    keep_ref[...] = jnp.where(first, low, high)
    send_ref[...] = jnp.where(first, high, low)
    lane = lax.broadcasted_iota(jnp.int32, energy_ref.shape, 1)
    energy_ref[...] = jnp.where(lane == 0, near_ref[...] + far_ref[...], jnp.full(energy_ref.shape, 2.0 * jnp.sum(energy)))


def in_vmem(count):
    return [pl.BlockSpec(memory_space=pltpu.VMEM)] * count


def in_smem(count):
    return [pl.BlockSpec(memory_space=pltpu.SMEM)] * count


def on_device(orbitals, kernel, occupations, plan):
    own, points, cells = orbitals.shape
    total_orbitals = occupations.shape[0]
    groups = lax.axis_size(PAIR)
    cores = lax.axis_size("core")
    chips = lax.axis_size("zl")
    slots = plan.shape[0] // groups
    column = lax.axis_size(("y", "x"))
    zh, zl, core = lax.axis_index("zh"), lax.axis_index("zl"), lax.axis_index("core")
    here = lax.axis_index(("y", "x"))
    steps = np.array([[dy * SIZES[2] + dx for dy, dx in chip] for chip in STEPS], np.int32)
    chip = jnp.where(zh == 0, zl, chips - 1 - zl)
    near_step = jnp.asarray(steps)[chip]
    step = near_step[core]
    owner = zh * column + here
    who = jnp.stack([owner, zh * column + (here ^ step), (1 - zh) * column + (here ^ step), core]).astype(jnp.int32)

    far = lax.ppermute(orbitals, AXES, routes(other_half))
    near = lax.ppermute(orbitals, AXES, routes(same_half))

    table = tables(points, own, groups, cores)
    constants = [jnp.asarray(table[name]) for name in NAMES]
    rows = own * points
    flops = 2 * 3 * own * own * points * cells * (own * own * points + 384) * 2
    cost = pl.CostEstimate(flops=flops, bytes_accessed=4 << 20, transcendentals=0)
    exchange, energy = pl.pallas_call(
        first_body,
        out_shape=(
            jax.ShapeDtypeStruct((rows, cells), jnp.float32),
            jax.ShapeDtypeStruct((8, 128), jnp.float32),
        ),
        in_specs=in_smem(2) + in_vmem(3 + len(NAMES)),
        out_specs=tuple(in_vmem(2)),
        cost_estimate=cost,
        name="near_pairs",
    )(who, occupations, orbitals, near, kernel, *constants)
    across = lax.ppermute(energy, AXES, routes(mirror))
    keep, send, energy = pl.pallas_call(
        second_body,
        out_shape=(
            jax.ShapeDtypeStruct((rows // 2, cells), jnp.float32),
            jax.ShapeDtypeStruct((rows // 2, cells), jnp.float32),
            jax.ShapeDtypeStruct((8, 128), jnp.float32),
        ),
        in_specs=in_smem(2) + in_vmem(6 + len(NAMES)),
        out_specs=tuple(in_vmem(3)),
        cost_estimate=cost,
        name="far_pairs",
    )(who, occupations, orbitals, far, kernel, *constants, exchange, energy, across)

    everyone = lax.all_to_all(
        jnp.broadcast_to(energy[:1, :], (column * cores, 128)), ("y", "x", "core"), 0, 0, tiled=True
    )
    received = lax.ppermute(send, AXES, routes(other_core))

    total = everyone[:, :2].reshape(column, cores, 2)
    while total.shape[0] > 1:
        half = total.shape[0] // 2
        total = total[:half] + total[half:]
    total = total[0]
    lane = jnp.arange(128, dtype=jnp.int32)
    levels = jnp.zeros((128,), jnp.float32)
    for at in range(cores):
        levels = levels + jnp.where(lane == near_step[at], total[at, 0], 0.0)
        levels = levels + jnp.where(lane == column + near_step[at], total[at, 1], 0.0)
    each = rows // 2 // chips
    summed = (keep + received).reshape(chips, each, cells)
    extra = jnp.broadcast_to(levels, (chips, each, 128))
    pieces = lax.all_to_all(jnp.concatenate([summed, extra], axis=2), "zl", 0, 0, tiled=True)
    result = jnp.sum(pieces, axis=0)
    exchange = result[:, :cells].reshape(own, each // own, cells)
    group = lax.axis_index(PAIR)
    mine_slots = lax.dynamic_slice_in_dim(plan, group * slots, slots)
    picked = jnp.where(lane[None] == mine_slots[:, None], result[:1, cells:], 0.0)
    slot_energy = -jnp.sum(picked, axis=1) / (2.0 * total_orbitals * points**3)
    return exchange, slot_energy


def solution(mesh):
    split_mesh = Mesh(mesh.devices.reshape(SIZES), AXES)
    return jax.shard_map(
        on_device,
        mesh=split_mesh,
        in_specs=(P(BAND, None, None), P(), P(), P()),
        out_specs=(P(BAND, PAIR, None), P(PAIR)),
        check_vma=False,
    )
```

```python
import functools
import math

import jax
import jax.numpy as jnp
import ml_dtypes
import numpy as np
from jax import lax
from jax.experimental import pallas as pl
from jax.experimental.pallas import tpu as pltpu
from jax.sharding import Mesh
from jax.sharding import PartitionSpec as P

AXES = ("zh", "y", "x", "zl", "core")
BAND = ("zh", "y", "x")
PAIR = ("zl", "core")
SIZES = (2, 4, 4, 8, 2)

STEPS = (
    ((2, 2), (2, 1)),
    ((2, 3), (3, 2)),
    ((3, 3), (3, 1)),
    ((0, 0), (1, 0)),
    ((0, 1), (0, 3)),
    ((1, 3), (1, 1)),
    ((0, 2), (3, 0)),
    ((1, 2), (2, 0)),
)


def step_of(zh, zl, core):
    return STEPS[zl if zh == 0 else SIZES[3] - 1 - zl][core]


def place(coords):
    flat = 0
    for size, at in zip(SIZES, coords):
        flat = flat * size + at
    return flat


def routes(move):
    return [(place(c), place(move(*c))) for c in np.ndindex(*SIZES)]


def same_half(zh, y, x, zl, core):
    dy, dx = step_of(zh, zl, core)
    return zh, y ^ dy, x ^ dx, zl, core


def other_half(zh, y, x, zl, core):
    dy, dx = step_of(zh, zl, core)
    return 1 - zh, y ^ dy, x ^ dx, SIZES[3] - 1 - zl, core


def mirror(zh, y, x, zl, core):
    return 1 - zh, y, x, SIZES[3] - 1 - zl, core


def other_core(zh, y, x, zl, core):
    return zh, y, x, zl, 1 - core


def two_parts(matrix):
    high = matrix.astype(ml_dtypes.bfloat16)
    low = (matrix - high.astype(np.float64)).astype(ml_dtypes.bfloat16)
    return np.stack([high, low])


def hartley(points):
    at = np.arange(points)
    angle = (np.outer(at, at) % points) * (2.0 * math.pi / points)
    return (np.cos(angle) + np.sin(angle)) / math.sqrt(points)


def mode_order(points):
    at = np.arange(points)
    return np.concatenate([at[0::4], at[2::4], at[1::2]])


@functools.cache
def tables(points, own, groups, cores):
    base = hartley(points)
    quarter = base[:, : points // 4]
    quarters = np.kron(quarter[0::4].T, base)
    halves = np.kron(quarter[2::4].T, base)
    odd = np.kron(base[1::2, : points // 2].T, base)
    pairs = own * own
    along = np.kron(np.eye(pairs), base)
    planes = points // groups
    rows = []
    for core in range(cores):
        for zl in range(groups // cores):
            for a in range(own):
                for low in range(planes):
                    rows.append((a, (zl * cores + core) * planes + low))
    picks = []
    spread = np.zeros((pairs * points, own * points))
    for b in range(own):
        for a, plane in rows:
            spread[len(picks), b * points + plane] = 1.0
            picks.append((b * own + a) * points + plane)
    return dict(
        along=two_parts(along).reshape(2 * pairs * points, pairs * points),
        back=two_parts(along[picks]).reshape(2 * pairs * points, pairs * points),
        spread=spread.astype(ml_dtypes.bfloat16),
        quarters=two_parts(quarters),
        halves=two_parts(halves),
        odd=two_parts(odd),
    )


NAMES = ("along", "back", "spread", "quarters", "halves", "odd")


def split(value):
    high = value.astype(jnp.bfloat16)
    return high, (value - high.astype(jnp.float32)).astype(jnp.bfloat16)


def product(left, right, contract):
    return lax.dot_general(left, right, (contract, ((), ())), preferred_element_type=jnp.float32)


def on_rows(value, matrix, contract):
    rows = value.shape[0]
    high, low = split(value)
    both = product(jnp.concatenate([high, low], axis=0), matrix[0], ((1,), (contract,)))
    rest = product(high, matrix[1], ((1,), (contract,)))
    return both[:rows] + both[rows:] + rest


def on_planes(matrix, value):
    rows = matrix.shape[0] // 2
    high, low = split(value)
    both = product(matrix, high, ((1,), (0,)))
    rest = product(matrix[:rows], low, ((1,), (0,)))
    return both[:rows] + both[rows:] + rest


def in_mode_order(kernel, points):
    order = mode_order(points)
    width = 128
    each = width // points
    lane = lax.broadcasted_iota(jnp.int32, (points, width), 1)
    columns = []
    for column in range(points * points // width):
        taken = None
        for at in range(each):
            source = int(order[column * each + at])
            block = kernel[:, source // each * width : (source // each + 1) * width]
            shift = (at - source % each) * points % width
            if shift:
                block = pltpu.roll(block, shift, 1)
            taken = block if taken is None else jnp.where(lane >= at * points, block, taken)
        columns.append(taken)
    return jnp.concatenate(columns, axis=1)


def pair_terms(mine, partner, mine_weight, partner_weight, kernel, table):
    own, points, cells = mine.shape
    pairs = own * own
    block = cells // 4
    left = mine.astype(jnp.float32)
    right = partner.astype(jnp.float32)
    modal = in_mode_order(kernel, points)
    along, back, spread = table["along"], table["back"], table["spread"]
    parts = []
    for at in range(4):
        lanes = slice(at * block, (at + 1) * block)
        density = jnp.concatenate(
            [left[a, :, lanes] * right[b, :, lanes] for b in range(own) for a in range(own)], axis=0
        )
        parts.append(on_planes(along, density))
    even0, even1 = parts[0] + parts[2], parts[1] + parts[3]
    odd = jnp.concatenate([parts[0] - parts[2], parts[1] - parts[3]], axis=1)
    spectrum = jnp.concatenate(
        [
            on_rows(even0 + even1, table["quarters"], 0),
            on_rows(even0 - even1, table["halves"], 0),
            on_rows(odd, table["odd"], 0),
        ],
        axis=1,
    )
    energies = []
    shaped = []
    for f in range(pairs):
        rows = spectrum[f * points : (f + 1) * points]
        potential = rows * modal
        shaped.append(potential)
        terms = (rows * potential).reshape(points // 8, 8, cells // 128, 128)
        energies.append(jnp.sum(terms, axis=(0, 2)))
    energy = jnp.zeros((8, 128), jnp.float32)
    straight = jnp.zeros((8, 128), jnp.float32)
    crossed = jnp.zeros((8, 128), jnp.float32)
    for b in range(own):
        for a in range(own):
            term = energies[b * own + a] * (mine_weight[a] * partner_weight[b])
            if a == b:
                straight = straight + term
            else:
                crossed = crossed + term
    energy = straight + crossed
    shaped = jnp.concatenate(shaped, axis=0)
    quarters = on_rows(shaped[:, :block], table["quarters"], 1)
    halves = on_rows(shaped[:, block : 2 * block], table["halves"], 1)
    odd = on_rows(shaped[:, 2 * block :], table["odd"], 1)
    even0, even1 = quarters + halves, quarters - halves
    odd0, odd1 = odd[:, :block], odd[:, block:]
    fields = [even0 + odd0, even1 + odd1, even0 - odd0, even1 - odd1]
    flat = partner.reshape(own * points, cells)
    rows = own * points
    pulled = []
    for at in range(4):
        potential = on_planes(back, fields[at])
        spreads = product(spread, flat[:, at * block : (at + 1) * block], ((1,), (0,)))
        total = None
        for b in range(own):
            term = potential[b * rows : (b + 1) * rows] * spreads[b * rows : (b + 1) * rows]
            term = term * partner_weight[b]
            total = term if total is None else total + term
        pulled.append(-total)
    return jnp.concatenate(pulled, axis=1), energy


def weights_of(occupation_ref, owner, own):
    return [occupation_ref[owner * own + at] for at in range(own)]


def whereabouts(steps_ref):
    zh, zl, core = lax.axis_index("zh"), lax.axis_index("zl"), lax.axis_index("core")
    here = lax.axis_index("y") * SIZES[2] + lax.axis_index("x")
    column = SIZES[1] * SIZES[2]
    chip = jnp.where(zh == 0, zl, SIZES[3] - 1 - zl)
    step = steps_ref[chip * SIZES[4] + core]
    there = jnp.bitwise_xor(here, step)
    return core, step, zh * column + here, zh * column + there, (1 - zh) * column + there


def first_body(steps_ref, occupation_ref, mine_ref, partner_ref, kernel_ref, *refs):
    table = {name: ref[...] for name, ref in zip(NAMES, refs)}
    exchange_ref, energy_ref = refs[len(NAMES) :]
    own = mine_ref.shape[0]
    _, _, owner, near, _ = whereabouts(steps_ref)
    exchange, energy = pair_terms(
        mine_ref[...],
        partner_ref[...],
        weights_of(occupation_ref, owner, own),
        weights_of(occupation_ref, near, own),
        kernel_ref[...],
        table,
    )
    exchange_ref[...] = exchange
    energy_ref[...] = jnp.full(energy_ref.shape, jnp.sum(energy))


def second_body(steps_ref, occupation_ref, mine_ref, partner_ref, kernel_ref, *refs):
    table = {name: ref[...] for name, ref in zip(NAMES, refs)}
    before_ref, near_ref, across_ref, keep_ref, send_ref, energy_ref = refs[len(NAMES) :]
    own = mine_ref.shape[0]
    core, step, owner, _, far = whereabouts(steps_ref)
    exchange, energy = pair_terms(
        mine_ref[...],
        partner_ref[...],
        weights_of(occupation_ref, owner, own),
        weights_of(occupation_ref, far, own),
        kernel_ref[...],
        table,
    )
    exchange = exchange + before_ref[...]
    half = exchange.shape[0] // 2
    low, high = exchange[:half], exchange[half:]
    keep_ref[...] = jnp.where(core == 0, low, high)
    send_ref[...] = jnp.where(core == 0, high, low)
    lane = lax.broadcasted_iota(jnp.int32, near_ref.shape, 1)
    near_total = near_ref[...] + across_ref[...]
    far_total = jnp.full(near_ref.shape, 2.0 * jnp.sum(energy))
    row = jnp.where(lane == step, near_total, jnp.where(lane == SIZES[1] * SIZES[2] + step, far_total, 0.0))
    energy_ref[...] = jnp.broadcast_to(row[None], energy_ref.shape)


def join_body(keep_ref, received_ref, energies_ref, out_ref):
    chips, each, width = out_ref.shape
    cells = keep_ref.shape[1]
    rows = energies_ref[:, 0, :]
    while rows.shape[0] > 8:
        half = rows.shape[0] // 2
        rows = rows[:half] + rows[half:]
    for shift in (4, 2, 1):
        rows = rows + pltpu.roll(rows, shift, 0)
    out_ref[:, :, :cells] = (keep_ref[...] + received_ref[...]).reshape(chips, each, cells)
    out_ref[:, :, cells:] = jnp.broadcast_to(rows[None, :each], (chips, each, width - cells))


def last_body(scale, plan_ref, pieces_ref, exchange_ref, slot_ref):
    chips, each, width = pieces_ref.shape
    own, planes, cells = exchange_ref.shape
    total = pieces_ref[0]
    for chip in range(1, chips):
        total = total + pieces_ref[chip]
    for a in range(own):
        exchange_ref[a] = total[a * planes : (a + 1) * planes, :cells]
    levels = total[:1, cells:]
    lane = lax.broadcasted_iota(jnp.int32, levels.shape, 1)
    slots = slot_ref.shape[0]
    group = lax.axis_index("zl") * SIZES[4] + lax.axis_index("core")
    for slot in range(slots):
        level = plan_ref[group * slots + slot]
        slot_ref[slot] = jnp.sum(jnp.where(lane == level, levels, 0.0)) * scale


def in_vmem(count):
    return [pl.BlockSpec(memory_space=pltpu.VMEM)] * count


def in_smem(count):
    return [pl.BlockSpec(memory_space=pltpu.SMEM)] * count


def floats(*shape):
    return jax.ShapeDtypeStruct(shape, jnp.float32)


PARAMS = pltpu.CompilerParams(vmem_limit_bytes=24 << 20)


def on_device(orbitals, kernel, occupations, plan):
    own, points, cells = orbitals.shape
    total_orbitals = occupations.shape[0]
    groups = lax.axis_size(PAIR)
    cores = lax.axis_size("core")
    chips = lax.axis_size("zl")
    slots = plan.shape[0] // groups
    column = lax.axis_size(("y", "x"))

    near = lax.ppermute(orbitals, AXES, routes(same_half))
    far = lax.ppermute(orbitals, AXES, routes(other_half))

    table = tables(points, own, groups, cores)
    steps = jnp.asarray(np.array([dy * SIZES[2] + dx for chip in STEPS for dy, dx in chip], np.int32))
    constants = [jnp.asarray(table[name]) for name in NAMES]
    rows = own * points
    each = rows // 2 // chips
    flops = 2 * 3 * own * own * points * cells * (own * own * points + 384) * 2
    cost = pl.CostEstimate(flops=flops, bytes_accessed=4 << 20, transcendentals=0)
    exchange, energy = pl.pallas_call(
        first_body,
        out_shape=(floats(rows, cells), floats(1, 128)),
        in_specs=in_smem(2) + in_vmem(3 + len(NAMES)),
        out_specs=tuple(in_vmem(2)),
        cost_estimate=cost,
        compiler_params=PARAMS,
        name="near_pairs",
    )(steps, occupations, orbitals, near, kernel, *constants)
    across = lax.ppermute(energy, AXES, routes(mirror))
    keep, send, energies = pl.pallas_call(
        second_body,
        out_shape=(floats(rows // 2, cells), floats(rows // 2, cells), floats(column * cores, 1, 128)),
        in_specs=in_smem(2) + in_vmem(6 + len(NAMES)),
        out_specs=tuple(in_vmem(3)),
        cost_estimate=cost,
        compiler_params=PARAMS,
        name="far_pairs",
    )(steps, occupations, orbitals, far, kernel, *constants, exchange, energy, across)

    everyone = lax.all_to_all(energies, ("y", "x", "core"), 0, 0, tiled=True)
    received = lax.ppermute(send, AXES, routes(other_core))
    joined = pl.pallas_call(
        join_body,
        out_shape=floats(chips, each, cells + 128),
        in_specs=in_vmem(3),
        out_specs=in_vmem(1)[0],
        compiler_params=PARAMS,
        name="join",
    )(keep, received, everyone)
    pieces = lax.all_to_all(joined, "zl", 0, 0, tiled=True)
    return pl.pallas_call(
        functools.partial(last_body, -1.0 / (2.0 * total_orbitals * points**3)),
        out_shape=(floats(own, each // own, cells), floats(slots)),
        in_specs=in_smem(1) + in_vmem(1),
        out_specs=(in_vmem(1)[0], in_smem(1)[0]),
        compiler_params=PARAMS,
        name="last",
    )(plan, pieces)


def solution(mesh):
    split_mesh = Mesh(mesh.devices.reshape(SIZES), AXES)
    return jax.shard_map(
        on_device,
        mesh=split_mesh,
        in_specs=(P(BAND, None, None), P(), P(), P()),
        out_specs=(P(BAND, PAIR, None), P(PAIR)),
        check_vma=False,
    )
```

```python
import functools
import math

import jax
import jax.numpy as jnp
import ml_dtypes
import numpy as np
from jax import lax
from jax.experimental import pallas as pl
from jax.experimental.pallas import tpu as pltpu
from jax.sharding import Mesh
from jax.sharding import PartitionSpec as P

AXES = ("zh", "y", "x", "zl", "core")
BAND = ("zh", "y", "x")
PAIR = ("zl", "core")
SIZES = (2, 4, 4, 8, 2)

STEPS = (
    ((2, 2), (2, 1)),
    ((2, 3), (3, 2)),
    ((3, 3), (3, 1)),
    ((0, 0), (1, 0)),
    ((0, 1), (0, 3)),
    ((1, 3), (1, 1)),
    ((0, 2), (3, 0)),
    ((1, 2), (2, 0)),
)


def step_of(zh, zl, core):
    return STEPS[zl if zh == 0 else SIZES[3] - 1 - zl][core]


def place(coords):
    flat = 0
    for size, at in zip(SIZES, coords):
        flat = flat * size + at
    return flat


def routes(move):
    return [(place(c), place(move(*c))) for c in np.ndindex(*SIZES)]


def same_half(zh, y, x, zl, core):
    dy, dx = step_of(zh, zl, core)
    return zh, y ^ dy, x ^ dx, zl, core


def other_half(zh, y, x, zl, core):
    dy, dx = step_of(zh, zl, core)
    return 1 - zh, y ^ dy, x ^ dx, SIZES[3] - 1 - zl, core


def mirror(zh, y, x, zl, core):
    return 1 - zh, y, x, SIZES[3] - 1 - zl, core


def other_core(zh, y, x, zl, core):
    return zh, y, x, zl, 1 - core


def two_parts(matrix):
    high = matrix.astype(ml_dtypes.bfloat16)
    low = (matrix - high.astype(np.float64)).astype(ml_dtypes.bfloat16)
    return np.stack([high, low])


def hartley(points):
    at = np.arange(points)
    angle = (np.outer(at, at) % points) * (2.0 * math.pi / points)
    return (np.cos(angle) + np.sin(angle)) / math.sqrt(points)


def mode_order(points):
    at = np.arange(points)
    return np.concatenate([at[0::4], at[2::4], at[1::2]])


@functools.cache
def tables(points, own, groups, cores):
    base = hartley(points)
    quarter = base[:, : points // 4]
    quarters = np.kron(quarter[0::4].T, base)
    halves = np.kron(quarter[2::4].T, base)
    odd = np.kron(base[1::2, : points // 2].T, base)
    pairs = own * own
    along = np.kron(np.eye(pairs), base)
    planes = points // groups
    rows = []
    for core in range(cores):
        for zl in range(groups // cores):
            for a in range(own):
                for low in range(planes):
                    rows.append((a, (zl * cores + core) * planes + low))
    picks = []
    spread = np.zeros((pairs * points, own * points))
    for b in range(own):
        for a, plane in rows:
            spread[len(picks), b * points + plane] = 1.0
            picks.append((b * own + a) * points + plane)
    square = lambda matrix: np.concatenate([two_parts(matrix)[part, :, at : at + 256] for part in range(2) for at in range(0, matrix.shape[1], 256)])
    sides = np.concatenate([two_parts(along).reshape(-1, pairs * points), two_parts(along[picks]).reshape(-1, pairs * points)], axis=1)
    blocks = [
        square(quarters),
        square(halves),
        square(odd),
        sides,
        np.pad(spread, ((0, 0), (0, 256 - spread.shape[1]))).astype(ml_dtypes.bfloat16),
    ]
    return np.concatenate(blocks)


def unpacked(ref, own, points):
    side = own * own * points
    big = [jnp.concatenate([ref[1024 + 512 * at : 1536 + 512 * at] for at in pair], axis=1) for pair in ((0, 1), (2, 3))]
    return dict(
        quarters=(ref[0:256], ref[256:512]),
        halves=(ref[512:768], ref[768:1024]),
        odd=big,
        along=ref[3072 : 3072 + 2 * side, :side],
        back=ref[3072 : 3072 + 2 * side, side : 2 * side],
        spread=ref[3072 + 2 * side : 3072 + 3 * side, : own * points],
    )


def split(value):
    high = value.astype(jnp.bfloat16)
    return high, (value - high.astype(jnp.float32)).astype(jnp.bfloat16)


def product(left, right, contract):
    return lax.dot_general(left, right, (contract, ((), ())), preferred_element_type=jnp.float32)


def on_rows(value, matrix, contract):
    rows = value.shape[0]
    high, low = split(value)
    both = product(jnp.concatenate([high, low], axis=0), matrix[0], ((1,), (contract,)))
    rest = product(high, matrix[1], ((1,), (contract,)))
    return both[:rows] + both[rows:] + rest


def on_planes(matrix, value):
    rows = matrix.shape[0] // 2
    high, low = split(value)
    both = product(matrix, high, ((1,), (0,)))
    rest = product(matrix[:rows], low, ((1,), (0,)))
    return both[:rows] + both[rows:] + rest


def in_mode_order(kernel, points):
    order = mode_order(points)
    width = 128
    each = width // points
    lane = lax.broadcasted_iota(jnp.int32, (points, width), 1)
    columns = []
    for column in range(points * points // width):
        taken = None
        for at in range(each):
            source = int(order[column * each + at])
            block = kernel[:, source // each * width : (source // each + 1) * width]
            shift = (at - source % each) * points % width
            if shift:
                block = pltpu.roll(block, shift, 1)
            taken = block if taken is None else jnp.where(lane >= at * points, block, taken)
        columns.append(taken)
    return jnp.concatenate(columns, axis=1)


def pair_terms(mine, partner, mine_weight, partner_weight, modal, table):
    own, points, cells = mine.shape
    pairs = own * own
    block = cells // 4
    left = mine.astype(jnp.float32)
    right = partner.astype(jnp.float32)
    along, back, spread = table["along"], table["back"], table["spread"]
    parts = []
    for at in range(4):
        lanes = slice(at * block, (at + 1) * block)
        density = jnp.concatenate(
            [left[a, :, lanes] * right[b, :, lanes] for b in range(own) for a in range(own)], axis=0
        )
        parts.append(on_planes(along, density))
    even0, even1 = parts[0] + parts[2], parts[1] + parts[3]
    odd = jnp.concatenate([parts[0] - parts[2], parts[1] - parts[3]], axis=1)
    spectrum = jnp.concatenate(
        [
            on_rows(even0 + even1, table["quarters"], 0),
            on_rows(even0 - even1, table["halves"], 0),
            on_rows(odd, table["odd"], 0),
        ],
        axis=1,
    )
    energies = []
    shaped = []
    for f in range(pairs):
        rows = spectrum[f * points : (f + 1) * points]
        potential = rows * modal
        shaped.append(potential)
        terms = (rows * potential).reshape(points // 8, 8, cells // 128, 128)
        energies.append(jnp.sum(terms, axis=(0, 2)))
    energy = jnp.zeros((8, 128), jnp.float32)
    straight = jnp.zeros((8, 128), jnp.float32)
    crossed = jnp.zeros((8, 128), jnp.float32)
    for b in range(own):
        for a in range(own):
            term = energies[b * own + a] * (mine_weight[a] * partner_weight[b])
            if a == b:
                straight = straight + term
            else:
                crossed = crossed + term
    energy = straight + crossed
    shaped = jnp.concatenate(shaped, axis=0)
    quarters = on_rows(shaped[:, :block], table["quarters"], 1)
    halves = on_rows(shaped[:, block : 2 * block], table["halves"], 1)
    odd = on_rows(shaped[:, 2 * block :], table["odd"], 1)
    even0, even1 = quarters + halves, quarters - halves
    odd0, odd1 = odd[:, :block], odd[:, block:]
    fields = [even0 + odd0, even1 + odd1, even0 - odd0, even1 - odd1]
    flat = partner.reshape(own * points, cells)
    rows = own * points
    pulled = []
    for at in range(4):
        potential = on_planes(back, fields[at])
        spreads = product(spread, flat[:, at * block : (at + 1) * block], ((1,), (0,)))
        total = None
        for b in range(own):
            term = potential[b * rows : (b + 1) * rows] * spreads[b * rows : (b + 1) * rows]
            term = term * partner_weight[b]
            total = term if total is None else total + term
        pulled.append(-total)
    return jnp.concatenate(pulled, axis=1), energy


def whereabouts():
    zh, zl, core = lax.axis_index("zh"), lax.axis_index("zl"), lax.axis_index("core")
    here = lax.axis_index("y") * SIZES[2] + lax.axis_index("x")
    column = SIZES[1] * SIZES[2]
    slot = jnp.where(zh == 0, zl, SIZES[3] - 1 - zl) * SIZES[4] + core
    step = jnp.int32(0)
    for at, (dy, dx) in enumerate(pair for chip in STEPS for pair in chip):
        step = jnp.where(slot == at, dy * SIZES[2] + dx, step)
    there = jnp.bitwise_xor(here, step)
    return step, zh * column + here, zh * column + there, (1 - zh) * column + there


def prep_body(occupation_ref, kernel_ref, modal_ref, notes_ref):
    step, *owners = whereabouts()
    lane = lax.broadcasted_iota(jnp.int32, (1, notes_ref.shape[1]), 1)
    row = 0
    for owner in owners:
        for at in range(2):
            notes_ref[row : row + 1] = jnp.full(lane.shape, occupation_ref[owner * 2 + at])
            row += 1
    notes_ref[row : row + 1] = jnp.where(lane == step, 1.0, 0.0)
    notes_ref[row + 1 : row + 2] = jnp.where(lane == SIZES[1] * SIZES[2] + step, 2.0, 0.0)
    modal_ref[...] = in_mode_order(kernel_ref[...], kernel_ref.shape[0])


def weights_of(notes_ref, which, own):
    return [notes_ref[which * own + at : which * own + at + 1, 0:1] for at in range(own)]


def first_body(partner_ref, mine_ref, table_ref, modal_ref, notes_ref, exchange_ref, energy_ref):
    own, points, _ = mine_ref.shape
    table = unpacked(table_ref, own, points)
    exchange, energy = pair_terms(
        mine_ref[...],
        partner_ref[...],
        weights_of(notes_ref, 0, own),
        weights_of(notes_ref, 1, own),
        modal_ref[...],
        table,
    )
    exchange_ref[...] = exchange
    energy_ref[...] = jnp.full(energy_ref.shape, jnp.sum(energy))


def second_body(
    partner_ref, mine_ref, table_ref, modal_ref, notes_ref, before_ref, near_ref, across_ref, keep_ref, send_ref, energy_ref
):
    own, points, _ = mine_ref.shape
    table = unpacked(table_ref, own, points)
    exchange, energy = pair_terms(
        mine_ref[...],
        partner_ref[...],
        weights_of(notes_ref, 0, own),
        weights_of(notes_ref, 2, own),
        modal_ref[...],
        table,
    )
    exchange = exchange + before_ref[...]
    half = exchange.shape[0] // 2
    low, high = exchange[:half], exchange[half:]
    core = lax.axis_index("core")
    keep_ref[...] = jnp.where(core == 0, low, high)
    send_ref[...] = jnp.where(core == 0, high, low)
    near_row = notes_ref[3 * own : 3 * own + 1]
    far_row = notes_ref[3 * own + 1 : 3 * own + 2]
    row = (near_ref[...] + across_ref[...]) * near_row + jnp.sum(energy) * far_row
    energy_ref[...] = jnp.broadcast_to(row[None], energy_ref.shape)


def join_body(keep_ref, received_ref, energies_ref, out_ref):
    chips, each, width = out_ref.shape
    cells = keep_ref.shape[1]
    rows = energies_ref[:, 0, :]
    while rows.shape[0] > 8:
        half = rows.shape[0] // 2
        rows = rows[:half] + rows[half:]
    for shift in (4, 2, 1):
        rows = rows + pltpu.roll(rows, shift, 0)
    out_ref[:, :, :cells] = (keep_ref[...] + received_ref[...]).reshape(chips, each, cells)
    out_ref[:, :, cells:] = jnp.broadcast_to(rows[None, :each], (chips, each, width - cells))


def last_body(scale, plan_ref, pieces_ref, exchange_ref, slot_ref):
    chips, each, width = pieces_ref.shape
    own, planes, cells = exchange_ref.shape
    total = pieces_ref[0]
    for chip in range(1, chips):
        total = total + pieces_ref[chip]
    for a in range(own):
        exchange_ref[a] = total[a * planes : (a + 1) * planes, :cells]
    levels = total[:1, cells:]
    lane = lax.broadcasted_iota(jnp.int32, levels.shape, 1)
    slots = slot_ref.shape[0]
    group = lax.axis_index("zl") * SIZES[4] + lax.axis_index("core")
    for slot in range(slots):
        level = plan_ref[group * slots + slot]
        slot_ref[slot] = jnp.sum(jnp.where(lane == level, levels, 0.0)) * scale


def in_vmem(count):
    return [pl.BlockSpec(memory_space=pltpu.VMEM)] * count


def in_smem(count):
    return [pl.BlockSpec(memory_space=pltpu.SMEM)] * count


def floats(*shape):
    return jax.ShapeDtypeStruct(shape, jnp.float32)


PARAMS = pltpu.CompilerParams(vmem_limit_bytes=24 << 20)


def on_device(orbitals, kernel, occupations, plan):
    own, points, cells = orbitals.shape
    total_orbitals = occupations.shape[0]
    groups = lax.axis_size(PAIR)
    cores = lax.axis_size("core")
    chips = lax.axis_size("zl")
    slots = plan.shape[0] // groups
    column = lax.axis_size(("y", "x"))

    near = lax.ppermute(orbitals, AXES, routes(same_half))
    far = lax.ppermute(orbitals, AXES, routes(other_half))

    table = jnp.asarray(tables(points, own, groups, cores))
    modal, notes = pl.pallas_call(
        prep_body,
        out_shape=(floats(points, cells), floats(8, 128)),
        in_specs=in_smem(1) + in_vmem(1),
        out_specs=tuple(in_vmem(2)),
        cost_estimate=pl.CostEstimate(flops=1 << 30, bytes_accessed=4 << 20, transcendentals=0),
        compiler_params=PARAMS,
        name="prep",
    )(occupations, kernel)
    ready = (orbitals, table, modal, notes)
    rows = own * points
    each = rows // 2 // chips
    flops = 2 * 3 * own * own * points * cells * (own * own * points + 384) * 2
    cost = pl.CostEstimate(flops=flops, bytes_accessed=4 << 20, transcendentals=0)
    exchange, energy = pl.pallas_call(
        first_body,
        out_shape=(floats(rows, cells), floats(1, 128)),
        in_specs=in_vmem(1 + len(ready)),
        out_specs=tuple(in_vmem(2)),
        cost_estimate=cost,
        compiler_params=PARAMS,
        name="near_pairs",
    )(near, *ready)
    across = lax.ppermute(energy, AXES, routes(mirror))
    keep, send, energies = pl.pallas_call(
        second_body,
        out_shape=(floats(rows // 2, cells), floats(rows // 2, cells), floats(column * cores, 1, 128)),
        in_specs=in_vmem(4 + len(ready)),
        out_specs=tuple(in_vmem(3)),
        cost_estimate=cost,
        compiler_params=PARAMS,
        name="far_pairs",
    )(far, *ready, exchange, energy, across)

    everyone = lax.all_to_all(energies, ("y", "x", "core"), 0, 0, tiled=True)
    received = lax.ppermute(send, AXES, routes(other_core))
    joined = pl.pallas_call(
        join_body,
        out_shape=floats(chips, each, cells + 128),
        in_specs=in_vmem(3),
        out_specs=in_vmem(1)[0],
        compiler_params=PARAMS,
        name="join",
    )(keep, received, everyone)
    pieces = lax.all_to_all(joined, "zl", 0, 0, tiled=True)
    return pl.pallas_call(
        functools.partial(last_body, -1.0 / (2.0 * total_orbitals * points**3)),
        out_shape=(floats(own, each // own, cells), floats(slots)),
        in_specs=in_smem(1) + in_vmem(1),
        out_specs=(in_vmem(1)[0], in_smem(1)[0]),
        compiler_params=PARAMS,
        name="last",
    )(plan, pieces)


def solution(mesh):
    split_mesh = Mesh(mesh.devices.reshape(SIZES), AXES)
    return jax.shard_map(
        on_device,
        mesh=split_mesh,
        in_specs=(P(BAND, None, None), P(), P(), P()),
        out_specs=(P(BAND, PAIR, None), P(PAIR)),
        check_vma=False,
    )
```

```python
import functools
import math

import jax
import jax.numpy as jnp
import ml_dtypes
import numpy as np
from jax import lax
from jax.experimental import pallas as pl
from jax.experimental.pallas import tpu as pltpu
from jax.sharding import Mesh
from jax.sharding import PartitionSpec as P

AXES = ("zh", "y", "x", "zl", "core")
BAND = ("zh", "y", "x")
PAIR = ("zl", "core")
SIZES = (2, 4, 4, 8, 2)

STEPS = (
    ((2, 2), (2, 1)),
    ((2, 3), (3, 2)),
    ((3, 3), (3, 1)),
    ((0, 0), (1, 0)),
    ((0, 1), (0, 3)),
    ((1, 3), (1, 1)),
    ((0, 2), (3, 0)),
    ((1, 2), (2, 0)),
)


def step_of(zh, zl, core):
    return STEPS[zl if zh == 0 else SIZES[3] - 1 - zl][core]


def place(coords):
    flat = 0
    for size, at in zip(SIZES, coords):
        flat = flat * size + at
    return flat


def routes(move):
    return [(place(c), place(move(*c))) for c in np.ndindex(*SIZES)]


def same_half(zh, y, x, zl, core):
    dy, dx = step_of(zh, zl, core)
    return zh, y ^ dy, x ^ dx, zl, core


def other_half(zh, y, x, zl, core):
    dy, dx = step_of(zh, zl, core)
    return 1 - zh, y ^ dy, x ^ dx, SIZES[3] - 1 - zl, core


def mirror(zh, y, x, zl, core):
    return 1 - zh, y, x, SIZES[3] - 1 - zl, core


def other_core(zh, y, x, zl, core):
    return zh, y, x, zl, 1 - core


def two_parts(matrix):
    high = matrix.astype(ml_dtypes.bfloat16)
    low = (matrix - high.astype(np.float64)).astype(ml_dtypes.bfloat16)
    return np.stack([high, low])


def hartley(points):
    at = np.arange(points)
    angle = (np.outer(at, at) % points) * (2.0 * math.pi / points)
    return (np.cos(angle) + np.sin(angle)) / math.sqrt(points)


def mode_order(points):
    at = np.arange(points)
    return np.concatenate([at[0::4], at[2::4], at[1::2]])


@functools.cache
def tables(points, own, groups, cores):
    base = hartley(points)
    quarter = base[:, : points // 4]
    quarters = np.kron(quarter[0::4].T, base)
    halves = np.kron(quarter[2::4].T, base)
    odd = np.kron(base[1::2, : points // 2].T, base)
    pairs = own * own
    along = np.kron(np.eye(pairs), base)
    planes = points // groups
    rows = []
    for core in range(cores):
        for zl in range(groups // cores):
            for a in range(own):
                for low in range(planes):
                    rows.append((a, (zl * cores + core) * planes + low))
    picks = []
    spread = np.zeros((pairs * points, own * points))
    for b in range(own):
        for a, plane in rows:
            spread[len(picks), b * points + plane] = 1.0
            picks.append((b * own + a) * points + plane)
    square = lambda matrix: np.concatenate([two_parts(matrix)[part, :, at : at + 256] for part in range(2) for at in range(0, matrix.shape[1], 256)])
    sides = np.concatenate([two_parts(along).reshape(-1, pairs * points), two_parts(along[picks]).reshape(-1, pairs * points)], axis=1)
    blocks = [
        square(quarters),
        square(halves),
        square(odd),
        sides,
        np.pad(spread, ((0, 0), (0, 256 - spread.shape[1]))).astype(ml_dtypes.bfloat16),
    ]
    return np.concatenate(blocks)


def unpacked(ref, own, points):
    side = own * own * points
    big = [jnp.concatenate([ref[1024 + 512 * at : 1536 + 512 * at] for at in pair], axis=1) for pair in ((0, 1), (2, 3))]
    return dict(
        quarters=(ref[0:256], ref[256:512]),
        halves=(ref[512:768], ref[768:1024]),
        odd=big,
        along=ref[3072 : 3072 + 2 * side, :side],
        back=ref[3072 : 3072 + 2 * side, side : 2 * side],
        spread=ref[3072 + 2 * side : 3072 + 3 * side, : own * points],
    )


def split(value):
    high = value.astype(jnp.bfloat16)
    return high, (value - high.astype(jnp.float32)).astype(jnp.bfloat16)


def product(left, right, contract):
    return lax.dot_general(left, right, (contract, ((), ())), preferred_element_type=jnp.float32)


def on_rows(value, matrix, contract):
    rows = value.shape[0]
    high, low = split(value)
    both = product(jnp.concatenate([high, low], axis=0), matrix[0], ((1,), (contract,)))
    rest = product(high, matrix[1], ((1,), (contract,)))
    return both[:rows] + both[rows:] + rest


def on_planes(matrix, value):
    rows = matrix.shape[0] // 2
    high, low = split(value)
    both = product(matrix, high, ((1,), (0,)))
    rest = product(matrix[:rows], low, ((1,), (0,)))
    return both[:rows] + both[rows:] + rest


def in_mode_order(kernel, points):
    order = mode_order(points)
    width = 128
    each = width // points
    lane = lax.broadcasted_iota(jnp.int32, (points, width), 1)
    columns = []
    for column in range(points * points // width):
        taken = None
        for at in range(each):
            source = int(order[column * each + at])
            block = kernel[:, source // each * width : (source // each + 1) * width]
            shift = (at - source % each) * points % width
            if shift:
                block = pltpu.roll(block, shift, 1)
            taken = block if taken is None else jnp.where(lane >= at * points, block, taken)
        columns.append(taken)
    return jnp.concatenate(columns, axis=1)


def forward(mine, partner, mine_weight, partner_weight, modal, table):
    own, points, cells = mine.shape
    pairs = own * own
    block = cells // 4
    left = mine.astype(jnp.float32)
    right = partner.astype(jnp.float32)
    along = table["along"]
    parts = []
    for at in range(4):
        lanes = slice(at * block, (at + 1) * block)
        density = jnp.concatenate(
            [left[a, :, lanes] * right[b, :, lanes] for b in range(own) for a in range(own)], axis=0
        )
        parts.append(on_planes(along, density))
    even0, even1 = parts[0] + parts[2], parts[1] + parts[3]
    odd = jnp.concatenate([parts[0] - parts[2], parts[1] - parts[3]], axis=1)
    spectrum = jnp.concatenate(
        [
            on_rows(even0 + even1, table["quarters"], 0),
            on_rows(even0 - even1, table["halves"], 0),
            on_rows(odd, table["odd"], 0),
        ],
        axis=1,
    )
    energies = []
    shaped = []
    for f in range(pairs):
        rows = spectrum[f * points : (f + 1) * points]
        potential = rows * modal
        shaped.append(potential)
        terms = (rows * potential).reshape(points // 8, 8, cells // 128, 128)
        energies.append(jnp.sum(terms, axis=(0, 2)))
    energy = jnp.zeros((8, 128), jnp.float32)
    straight = jnp.zeros((8, 128), jnp.float32)
    crossed = jnp.zeros((8, 128), jnp.float32)
    for b in range(own):
        for a in range(own):
            term = energies[b * own + a] * (mine_weight[a] * partner_weight[b])
            if a == b:
                straight = straight + term
            else:
                crossed = crossed + term
    energy = straight + crossed
    return jnp.concatenate(shaped, axis=0), energy


def backward(shaped, partners, weights, table):
    own, points, cells = partners[0].shape
    block = cells // 4
    rows = own * points
    quarters = on_rows(shaped[:, :block], table["quarters"], 1)
    halves = on_rows(shaped[:, block : 2 * block], table["halves"], 1)
    odd = on_rows(shaped[:, 2 * block :], table["odd"], 1)
    even0, even1 = quarters + halves, quarters - halves
    odd0, odd1 = odd[:, :block], odd[:, block:]
    fields = [even0 + odd0, even1 + odd1, even0 - odd0, even1 - odd1]
    pulled = []
    for at in range(4):
        total = None
        for turn, (partner, weight) in enumerate(zip(partners, weights)):
            potential = on_planes(table["back"], fields[at][turn * own * rows : (turn + 1) * own * rows])
            flat = partner.reshape(own * points, cells)[:, at * block : (at + 1) * block]
            spreads = product(table["spread"], flat, ((1,), (0,)))
            for b in range(own):
                term = potential[b * rows : (b + 1) * rows] * spreads[b * rows : (b + 1) * rows] * weight[b]
                total = term if total is None else total + term
        pulled.append(-total)
    return jnp.concatenate(pulled, axis=1)


def whereabouts():
    zh, zl, core = lax.axis_index("zh"), lax.axis_index("zl"), lax.axis_index("core")
    here = lax.axis_index("y") * SIZES[2] + lax.axis_index("x")
    column = SIZES[1] * SIZES[2]
    slot = jnp.where(zh == 0, zl, SIZES[3] - 1 - zl) * SIZES[4] + core
    step = jnp.int32(0)
    for at, (dy, dx) in enumerate(pair for chip in STEPS for pair in chip):
        step = jnp.where(slot == at, dy * SIZES[2] + dx, step)
    there = jnp.bitwise_xor(here, step)
    return step, zh * column + here, zh * column + there, (1 - zh) * column + there


def prep_body(occupation_ref, plan_ref, notes_ref):
    step, *owners = whereabouts()
    lane = lax.broadcasted_iota(jnp.int32, (1, notes_ref.shape[1]), 1)
    group = lax.axis_index("zl") * SIZES[4] + lax.axis_index("core")
    rows = [jnp.full(lane.shape, occupation_ref[owner * 2 + at]) for owner in owners for at in range(2)]
    levels = [step, SIZES[1] * SIZES[2] + step, plan_ref[group * 2], plan_ref[group * 2 + 1]]
    rows += [jnp.where(lane == level, 1.0, 0.0) for level in levels]
    for at, row in enumerate(rows):
        notes_ref[at : at + 1] = row


def weights_of(notes_ref, which, own):
    return [notes_ref[which * own + at : which * own + at + 1, 0:1] for at in range(own)]


NEAR, FAR = 1, 2


def forward_body(which, partner_ref, mine_ref, table_ref, kernel_ref, notes_ref, shaped_ref, energy_ref):
    own, points, _ = mine_ref.shape
    shaped, energy = forward(
        mine_ref[...],
        partner_ref[...],
        weights_of(notes_ref, 0, own),
        weights_of(notes_ref, which, own),
        in_mode_order(kernel_ref[...], points),
        unpacked(table_ref, own, points),
    )
    shaped_ref[...] = shaped
    energy_ref[...] = jnp.full(energy_ref.shape, jnp.sum(energy))


def back_body(near_ref, far_ref, table_ref, notes_ref, near_shaped_ref, far_shaped_ref, keep_ref, send_ref):
    own, points, _ = near_ref.shape
    exchange = backward(
        jnp.concatenate([near_shaped_ref[...], far_shaped_ref[...]], axis=0),
        [near_ref[...], far_ref[...]],
        [weights_of(notes_ref, which, own) for which in (NEAR, FAR)],
        unpacked(table_ref, own, points),
    )
    half = exchange.shape[0] // 2
    low, high = exchange[:half], exchange[half:]
    core = lax.axis_index("core")
    keep_ref[...] = jnp.where(core == 0, low, high)
    send_ref[...] = jnp.where(core == 0, high, low)


def rows_body(near_ref, across_ref, far_ref, notes_ref, out_ref):
    row = (near_ref[...] + across_ref[...]) * notes_ref[6:7] + 2.0 * far_ref[...] * notes_ref[7:8]
    out_ref[...] = jnp.broadcast_to(row[None], out_ref.shape)


def join_body(keep_ref, received_ref, energies_ref, out_ref):
    chips, each, width = out_ref.shape
    cells = keep_ref.shape[1]
    rows = energies_ref[:, 0, :]
    while rows.shape[0] > 8:
        half = rows.shape[0] // 2
        rows = rows[:half] + rows[half:]
    for shift in (4, 2, 1):
        rows = rows + pltpu.roll(rows, shift, 0)
    out_ref[:, :, :cells] = (keep_ref[...] + received_ref[...]).reshape(chips, each, cells)
    out_ref[:, :, cells:] = jnp.broadcast_to(rows[None, :each], (chips, each, width - cells))


def last_body(scale, notes_ref, pieces_ref, exchange_ref, slot_ref):
    chips, _, _ = pieces_ref.shape
    own, planes, cells = exchange_ref.shape
    total = pieces_ref[0]
    for chip in range(1, chips):
        total = total + pieces_ref[chip]
    for a in range(own):
        exchange_ref[a] = total[a * planes : (a + 1) * planes, :cells]
    levels = total[:1, cells:]
    for slot in range(slot_ref.shape[0]):
        slot_ref[slot] = jnp.sum(levels * notes_ref[8 + slot : 9 + slot]) * scale


def in_vmem(count):
    return [pl.BlockSpec(memory_space=pltpu.VMEM)] * count


def in_smem(count):
    return [pl.BlockSpec(memory_space=pltpu.SMEM)] * count


def floats(*shape):
    return jax.ShapeDtypeStruct(shape, jnp.float32)


PARAMS = pltpu.CompilerParams(vmem_limit_bytes=24 << 20)


def on_device(orbitals, kernel, occupations, plan):
    own, points, cells = orbitals.shape
    total_orbitals = occupations.shape[0]
    groups = lax.axis_size(PAIR)
    cores = lax.axis_size("core")
    chips = lax.axis_size("zl")
    slots = plan.shape[0] // groups
    column = lax.axis_size(("y", "x"))

    near = lax.ppermute(orbitals, AXES, routes(same_half))
    far = lax.ppermute(orbitals, AXES, routes(other_half))

    table = jnp.asarray(tables(points, own, groups, cores))
    rows = own * points
    each = rows // 2 // chips
    pairs = own * own

    def call(body, out_shape, *arrays, smem=0, smem_out=0, flops=0):
        count = len(out_shape) if isinstance(out_shape, tuple) else 0
        outs = in_vmem(max(count, 1) - smem_out) + in_smem(smem_out)
        return pl.pallas_call(
            body,
            out_shape=out_shape,
            in_specs=in_smem(smem) + in_vmem(len(arrays) - smem),
            out_specs=tuple(outs) if count else outs[0],
            cost_estimate=pl.CostEstimate(flops=flops, bytes_accessed=1 << 20, transcendentals=0),
            compiler_params=PARAMS,
        )(*arrays)

    notes = call(prep_body, floats(16, 128), occupations, plan, smem=2, flops=1 << 30)
    spectral = (floats(pairs * points, cells), floats(1, 128))
    work = 6 * pairs * points * cells * (pairs * points + 384)
    near_shaped, near_energy = call(
        functools.partial(forward_body, NEAR), spectral, near, orbitals, table, kernel, notes, flops=work
    )
    across = lax.ppermute(near_energy, AXES, routes(mirror))
    far_shaped, far_energy = call(
        functools.partial(forward_body, FAR), spectral, far, orbitals, table, kernel, notes, flops=work
    )
    energies = call(rows_body, floats(column * cores, 1, 128), near_energy, across, far_energy, notes)
    everyone = lax.all_to_all(energies, ("y", "x", "core"), 0, 0, tiled=True)
    half = floats(rows // 2, cells)
    keep, send = call(back_body, (half, half), near, far, table, notes, near_shaped, far_shaped, flops=2 * work)
    received = lax.ppermute(send, AXES, routes(other_core))
    joined = call(join_body, floats(chips, each, cells + 128), keep, received, everyone)
    pieces = lax.all_to_all(joined, "zl", 0, 0, tiled=True)
    scale = -1.0 / (2.0 * total_orbitals * points**3)
    outs = (floats(own, each // own, cells), floats(slots))
    return call(functools.partial(last_body, scale), outs, notes, pieces, smem_out=1)


def solution(mesh):
    split_mesh = Mesh(mesh.devices.reshape(SIZES), AXES)

    return jax.shard_map(
        on_device,
        mesh=split_mesh,
        in_specs=(P(BAND, None, None), P(), P(), P()),
        out_specs=(P(BAND, PAIR, None), P(PAIR)),
        check_vma=False,
    )
```

```python
import functools
import math

import jax
import jax.numpy as jnp
import ml_dtypes
import numpy as np
from jax import lax
from jax.experimental import pallas as pl
from jax.experimental.pallas import tpu as pltpu
from jax.sharding import Mesh
from jax.sharding import PartitionSpec as P

AXES = ("zh", "y", "x", "zl", "core")
BAND = ("zh", "y", "x")
PAIR = ("zl", "core")
SIZES = (2, 4, 4, 8, 2)

STEPS = (
    ((2, 2), (2, 1)),
    ((2, 3), (3, 2)),
    ((3, 3), (3, 1)),
    ((0, 0), (1, 0)),
    ((0, 1), (0, 3)),
    ((1, 3), (1, 1)),
    ((0, 2), (3, 0)),
    ((1, 2), (2, 0)),
)


def step_of(zh, zl, core):
    return STEPS[zl if zh == 0 else SIZES[3] - 1 - zl][core]


def place(coords):
    flat = 0
    for size, at in zip(SIZES, coords):
        flat = flat * size + at
    return flat


def routes(move, half=None):
    return [(place(c), place(move(*c))) for c in np.ndindex(*SIZES) if half in (None, c[0])]


def same_half(zh, y, x, zl, core):
    dy, dx = step_of(zh, zl, core)
    return zh, y ^ dy, x ^ dx, zl, core


def other_half(zh, y, x, zl, core):
    dy, dx = step_of(zh, zl, core)
    return 1 - zh, y ^ dy, x ^ dx, SIZES[3] - 1 - zl, core


def mirror(zh, y, x, zl, core):
    return 1 - zh, y, x, SIZES[3] - 1 - zl, core


def other_core(zh, y, x, zl, core):
    return zh, y, x, zl, 1 - core


def two_parts(matrix):
    high = matrix.astype(ml_dtypes.bfloat16)
    low = (matrix - high.astype(np.float64)).astype(ml_dtypes.bfloat16)
    return np.stack([high, low])


def hartley(points):
    at = np.arange(points)
    angle = (np.outer(at, at) % points) * (2.0 * math.pi / points)
    return (np.cos(angle) + np.sin(angle)) / math.sqrt(points)


def mode_order(points):
    at = np.arange(points)
    return np.concatenate([at[0::4], at[2::4], at[1::2]])


@functools.cache
def tables(points, own, groups, cores):
    base = hartley(points)
    quarter = base[:, : points // 4]
    quarters = np.kron(quarter[0::4].T, base)
    halves = np.kron(quarter[2::4].T, base)
    odd = np.kron(base[1::2, : points // 2].T, base)
    pairs = own * own
    along = np.kron(np.eye(pairs), base)
    planes = points // groups
    rows = []
    for core in range(cores):
        for zl in range(groups // cores):
            for a in range(own):
                for low in range(planes):
                    rows.append((a, (zl * cores + core) * planes + low))
    picks = []
    spread = np.zeros((pairs * points, own * points))
    for b in range(own):
        for a, plane in rows:
            spread[len(picks), b * points + plane] = 1.0
            picks.append((b * own + a) * points + plane)
    square = lambda matrix: np.concatenate([two_parts(matrix)[part, :, at : at + 256] for part in range(2) for at in range(0, matrix.shape[1], 256)])
    sides = np.concatenate([two_parts(along).reshape(-1, pairs * points), two_parts(along[picks]).reshape(-1, pairs * points)], axis=1)
    blocks = [
        square(quarters),
        square(halves),
        square(odd),
        sides,
        np.pad(spread, ((0, 0), (0, 256 - spread.shape[1]))).astype(ml_dtypes.bfloat16),
    ]
    return np.concatenate(blocks)


def unpacked(ref, own, points):
    side = own * own * points
    big = [jnp.concatenate([ref[1024 + 512 * at : 1536 + 512 * at] for at in pair], axis=1) for pair in ((0, 1), (2, 3))]
    return dict(
        quarters=(ref[0:256], ref[256:512]),
        halves=(ref[512:768], ref[768:1024]),
        odd=big,
        along=ref[3072 : 3072 + 2 * side, :side],
        back=ref[3072 : 3072 + 2 * side, side : 2 * side],
        spread=ref[3072 + 2 * side : 3072 + 3 * side, : own * points],
    )


def split(value):
    high = value.astype(jnp.bfloat16)
    return high, (value - high.astype(jnp.float32)).astype(jnp.bfloat16)


def product(left, right, contract):
    return lax.dot_general(left, right, (contract, ((), ())), preferred_element_type=jnp.float32)


def on_rows(value, matrix, contract):
    rows = value.shape[0]
    high, low = split(value)
    both = product(jnp.concatenate([high, low], axis=0), matrix[0], ((1,), (contract,)))
    rest = product(high, matrix[1], ((1,), (contract,)))
    return both[:rows] + both[rows:] + rest


def on_planes(matrix, value):
    rows = matrix.shape[0] // 2
    high, low = split(value)
    both = product(matrix, high, ((1,), (0,)))
    rest = product(matrix[:rows], low, ((1,), (0,)))
    return both[:rows] + both[rows:] + rest


def in_mode_order(kernel, points):
    order = mode_order(points)
    width = 128
    each = width // points
    lane = lax.broadcasted_iota(jnp.int32, (points, width), 1)
    columns = []
    for column in range(points * points // width):
        taken = None
        for at in range(each):
            source = int(order[column * each + at])
            block = kernel[:, source // each * width : (source // each + 1) * width]
            shift = (at - source % each) * points % width
            if shift:
                block = pltpu.roll(block, shift, 1)
            taken = block if taken is None else jnp.where(lane >= at * points, block, taken)
        columns.append(taken)
    return jnp.concatenate(columns, axis=1)


def forward(mine, partner, mine_weight, partner_weight, modal, table):
    own, points, cells = mine.shape
    pairs = own * own
    block = cells // 4
    left = mine.astype(jnp.float32)
    right = partner.astype(jnp.float32)
    along = table["along"]
    parts = []
    for at in range(4):
        lanes = slice(at * block, (at + 1) * block)
        density = jnp.concatenate(
            [left[a, :, lanes] * right[b, :, lanes] for b in range(own) for a in range(own)], axis=0
        )
        parts.append(on_planes(along, density))
    even0, even1 = parts[0] + parts[2], parts[1] + parts[3]
    odd = jnp.concatenate([parts[0] - parts[2], parts[1] - parts[3]], axis=1)
    spectrum = jnp.concatenate(
        [
            on_rows(even0 + even1, table["quarters"], 0),
            on_rows(even0 - even1, table["halves"], 0),
            on_rows(odd, table["odd"], 0),
        ],
        axis=1,
    )
    energies = []
    shaped = []
    for f in range(pairs):
        rows = spectrum[f * points : (f + 1) * points]
        potential = rows * modal
        shaped.append(potential)
        terms = (rows * potential).reshape(points // 8, 8, cells // 128, 128)
        energies.append(jnp.sum(terms, axis=(0, 2)))
    energy = jnp.zeros((8, 128), jnp.float32)
    straight = jnp.zeros((8, 128), jnp.float32)
    crossed = jnp.zeros((8, 128), jnp.float32)
    for b in range(own):
        for a in range(own):
            term = energies[b * own + a] * (mine_weight[a] * partner_weight[b])
            if a == b:
                straight = straight + term
            else:
                crossed = crossed + term
    energy = straight + crossed
    return jnp.concatenate(shaped, axis=0), energy


def backward(shaped, partners, weights, table):
    own, points, cells = partners[0].shape
    block = cells // 4
    rows = own * points
    quarters = on_rows(shaped[:, :block], table["quarters"], 1)
    halves = on_rows(shaped[:, block : 2 * block], table["halves"], 1)
    odd = on_rows(shaped[:, 2 * block :], table["odd"], 1)
    even0, even1 = quarters + halves, quarters - halves
    odd0, odd1 = odd[:, :block], odd[:, block:]
    fields = [even0 + odd0, even1 + odd1, even0 - odd0, even1 - odd1]
    pulled = []
    for at in range(4):
        total = None
        for turn, (partner, weight) in enumerate(zip(partners, weights)):
            potential = on_planes(table["back"], fields[at][turn * own * rows : (turn + 1) * own * rows])
            flat = partner.reshape(own * points, cells)[:, at * block : (at + 1) * block]
            spreads = product(table["spread"], flat, ((1,), (0,)))
            for b in range(own):
                term = potential[b * rows : (b + 1) * rows] * spreads[b * rows : (b + 1) * rows] * weight[b]
                total = term if total is None else total + term
        pulled.append(-total)
    return jnp.concatenate(pulled, axis=1)


def whereabouts():
    zh, zl, core = lax.axis_index("zh"), lax.axis_index("zl"), lax.axis_index("core")
    here = lax.axis_index("y") * SIZES[2] + lax.axis_index("x")
    column = SIZES[1] * SIZES[2]
    slot = jnp.where(zh == 0, zl, SIZES[3] - 1 - zl) * SIZES[4] + core
    step = jnp.int32(0)
    for at, (dy, dx) in enumerate(pair for chip in STEPS for pair in chip):
        step = jnp.where(slot == at, dy * SIZES[2] + dx, step)
    there = jnp.bitwise_xor(here, step)
    return step, zh * column + here, zh * column + there, (1 - zh) * column + there


def prep_body(occupation_ref, notes_ref):
    step, *owners = whereabouts()
    lane = lax.broadcasted_iota(jnp.int32, (1, notes_ref.shape[1]), 1)
    rows = [jnp.full(lane.shape, occupation_ref[owner * 2 + at]) for owner in owners for at in range(2)]
    rows += [jnp.where(lane == level, 1.0, 0.0) for level in (step, SIZES[1] * SIZES[2] + step)]
    for at, row in enumerate(rows):
        notes_ref[at : at + 1] = row


def picks_body(plan_ref, picks_ref):
    slots = picks_ref.shape[0]
    lane = lax.broadcasted_iota(jnp.int32, (1, picks_ref.shape[1]), 1)
    group = lax.axis_index("zl") * SIZES[4] + lax.axis_index("core")
    for slot in range(slots):
        picks_ref[slot : slot + 1] = jnp.where(lane == plan_ref[group * slots + slot], 1.0, 0.0)


def taken(first_ref, second_ref, first):
    return jnp.where(first, first_ref[...], second_ref[...])


def weights_of(notes_ref, which, own):
    return [notes_ref[which * own + at : which * own + at + 1, 0:1] for at in range(own)]


NEAR, FAR = 1, 2


def forward_body(which, low_ref, high_ref, mine_ref, table_ref, kernel_ref, notes_ref, shaped_ref, energy_ref, partner_ref):
    own, points, _ = mine_ref.shape
    partner = taken(low_ref, high_ref, lax.axis_index("zh") == 0)
    partner_ref[...] = partner
    shaped, energy = forward(
        mine_ref[...],
        partner,
        weights_of(notes_ref, 0, own),
        weights_of(notes_ref, which, own),
        in_mode_order(kernel_ref[...], points),
        unpacked(table_ref, own, points),
    )
    shaped_ref[...] = shaped
    energy_ref[...] = jnp.full(energy_ref.shape, jnp.sum(energy))


def back_body(near_ref, far_ref, table_ref, notes_ref, near_shaped_ref, far_shaped_ref, keep_ref, send_ref):
    own, points, _ = near_ref.shape
    exchange = backward(
        jnp.concatenate([near_shaped_ref[...], far_shaped_ref[...]], axis=0),
        [near_ref[...], far_ref[...]],
        [weights_of(notes_ref, which, own) for which in (NEAR, FAR)],
        unpacked(table_ref, own, points),
    )
    half = exchange.shape[0] // 2
    low, high = exchange[:half], exchange[half:]
    core = lax.axis_index("core")
    keep_ref[...] = jnp.where(core == 0, low, high)
    send_ref[...] = jnp.where(core == 0, high, low)


def rows_body(near_ref, across_ref, far_ref, notes_ref, out_ref):
    row = (near_ref[...] + across_ref[...]) * notes_ref[6:7] + 2.0 * far_ref[...] * notes_ref[7:8]
    out_ref[...] = jnp.broadcast_to(row[None], out_ref.shape)


def join_body(keep_ref, received_ref, energies_ref, out_ref):
    chips, each, width = out_ref.shape
    cells = keep_ref.shape[1]
    rows = energies_ref[:, 0, :]
    while rows.shape[0] > 8:
        half = rows.shape[0] // 2
        rows = rows[:half] + rows[half:]
    for shift in (4, 2, 1):
        rows = rows + pltpu.roll(rows, shift, 0)
    out_ref[:, :, :cells] = (keep_ref[...] + received_ref[...]).reshape(chips, each, cells)
    out_ref[:, :, cells:] = jnp.broadcast_to(rows[None, :each], (chips, each, width - cells))


def last_body(scale, picks_ref, pieces_ref, exchange_ref, slot_ref):
    chips, _, _ = pieces_ref.shape
    own, planes, cells = exchange_ref.shape
    total = pieces_ref[0]
    for chip in range(1, chips):
        total = total + pieces_ref[chip]
    for a in range(own):
        exchange_ref[a] = total[a * planes : (a + 1) * planes, :cells]
    levels = total[:1, cells:]
    for slot in range(slot_ref.shape[0]):
        slot_ref[slot] = jnp.sum(levels * picks_ref[slot : slot + 1]) * scale


def in_vmem(count):
    return [pl.BlockSpec(memory_space=pltpu.VMEM)] * count


def in_smem(count):
    return [pl.BlockSpec(memory_space=pltpu.SMEM)] * count


def floats(*shape):
    return jax.ShapeDtypeStruct(shape, jnp.float32)


PARAMS = pltpu.CompilerParams(vmem_limit_bytes=24 << 20)


def on_device(orbitals, kernel, occupations, plan):
    own, points, cells = orbitals.shape
    total_orbitals = occupations.shape[0]
    groups = lax.axis_size(PAIR)
    cores = lax.axis_size("core")
    chips = lax.axis_size("zl")
    slots = plan.shape[0] // groups
    column = lax.axis_size(("y", "x"))

    def moved(move, half):
        return lax.ppermute(orbitals, AXES, routes(move, half))

    far = [moved(other_half, 1), moved(other_half, 0)]
    near = [moved(same_half, 0), moved(same_half, 1)]

    table = jnp.asarray(tables(points, own, groups, cores))
    rows = own * points
    each = rows // 2 // chips
    pairs = own * own

    def call(body, out_shape, *arrays, smem=0, smem_out=0, flops=0):
        count = len(out_shape) if isinstance(out_shape, tuple) else 0
        outs = in_vmem(max(count, 1) - smem_out) + in_smem(smem_out)
        return pl.pallas_call(
            body,
            out_shape=out_shape,
            in_specs=in_smem(smem) + in_vmem(len(arrays) - smem),
            out_specs=tuple(outs) if count else outs[0],
            cost_estimate=pl.CostEstimate(flops=flops, bytes_accessed=1 << 20, transcendentals=0),
            compiler_params=PARAMS,
        )(*arrays)

    notes = call(prep_body, floats(8, 128), occupations, smem=1, flops=1 << 30)
    spectral = (floats(pairs * points, cells), floats(1, 128), jax.ShapeDtypeStruct(orbitals.shape, orbitals.dtype))
    work = 6 * pairs * points * cells * (pairs * points + 384)
    near_shaped, near_energy, near = call(
        functools.partial(forward_body, NEAR), spectral, *near, orbitals, table, kernel, notes, flops=work
    )
    across = lax.ppermute(near_energy, AXES, routes(mirror))
    picks = call(picks_body, floats(slots, 128), plan, smem=1)
    far_shaped, far_energy, far = call(
        functools.partial(forward_body, FAR), spectral, *far, orbitals, table, kernel, notes, flops=work
    )
    energies = call(rows_body, floats(column * cores, 1, 128), near_energy, across, far_energy, notes)
    everyone = lax.all_to_all(energies, ("y", "x", "core"), 0, 0, tiled=True)
    half = floats(rows // 2, cells)
    keep, send = call(back_body, (half, half), near, far, table, notes, near_shaped, far_shaped, flops=2 * work)
    received = lax.ppermute(send, AXES, routes(other_core))
    joined = call(join_body, floats(chips, each, cells + 128), keep, received, everyone)
    pieces = lax.all_to_all(joined, "zl", 0, 0, tiled=True)
    scale = -1.0 / (2.0 * total_orbitals * points**3)
    outs = (floats(own, each // own, cells), floats(slots))
    return call(functools.partial(last_body, scale), outs, picks, pieces, smem_out=1)


def solution(mesh):
    split_mesh = Mesh(mesh.devices.reshape(SIZES), AXES)

    return jax.shard_map(
        on_device,
        mesh=split_mesh,
        in_specs=(P(BAND, None, None), P(), P(), P()),
        out_specs=(P(BAND, PAIR, None), P(PAIR)),
        check_vma=False,
    )
```

```python
import functools
import math

import jax
import jax.numpy as jnp
import ml_dtypes
import numpy as np
from jax import lax
from jax.experimental import pallas as pl
from jax.experimental.pallas import tpu as pltpu
from jax.sharding import Mesh
from jax.sharding import PartitionSpec as P

AXES = ("zh", "y", "x", "zl", "core")
BAND = ("zh", "y", "x")
PAIR = ("zl", "core")
SIZES = (2, 4, 4, 8, 2)

STEPS = (
    ((2, 2), (2, 1)),
    ((2, 3), (3, 2)),
    ((3, 3), (3, 1)),
    ((0, 0), (1, 0)),
    ((0, 1), (0, 3)),
    ((1, 3), (1, 1)),
    ((0, 2), (3, 0)),
    ((1, 2), (2, 0)),
)


def step_of(zh, zl, core):
    return STEPS[zl if zh == 0 else SIZES[3] - 1 - zl][core]


def place(coords):
    flat = 0
    for size, at in zip(SIZES, coords):
        flat = flat * size + at
    return flat


def routes(move, half=None):
    return [(place(c), place(move(*c))) for c in np.ndindex(*SIZES) if half in (None, c[0])]


def same_half(zh, y, x, zl, core):
    dy, dx = step_of(zh, zl, core)
    return zh, y ^ dy, x ^ dx, zl, core


def other_half(zh, y, x, zl, core):
    dy, dx = step_of(zh, zl, core)
    return 1 - zh, y ^ dy, x ^ dx, SIZES[3] - 1 - zl, core


def mirror(zh, y, x, zl, core):
    return 1 - zh, y, x, SIZES[3] - 1 - zl, core


def other_core(zh, y, x, zl, core):
    return zh, y, x, zl, 1 - core


def two_parts(matrix):
    high = matrix.astype(ml_dtypes.bfloat16)
    low = (matrix - high.astype(np.float64)).astype(ml_dtypes.bfloat16)
    return np.stack([high, low])


def hartley(points):
    at = np.arange(points)
    angle = (np.outer(at, at) % points) * (2.0 * math.pi / points)
    return (np.cos(angle) + np.sin(angle)) / math.sqrt(points)


def mode_order(points):
    at = np.arange(points)
    return np.concatenate([at[0::4], at[2::4], at[1::2]])


@functools.cache
def tables(points, own, groups, cores):
    base = hartley(points)
    quarter = base[:, : points // 4]
    quarters = np.kron(quarter[0::4].T, base)
    halves = np.kron(quarter[2::4].T, base)
    odd = np.kron(base[1::2, : points // 2].T, base)
    pairs = own * own
    along = np.kron(np.eye(pairs), base)
    planes = points // groups
    rows = []
    for core in range(cores):
        for zl in range(groups // cores):
            for a in range(own):
                for low in range(planes):
                    rows.append((a, (zl * cores + core) * planes + low))
    picks = []
    spread = np.zeros((pairs * points, own * points))
    for b in range(own):
        for a, plane in rows:
            spread[len(picks), b * points + plane] = 1.0
            picks.append((b * own + a) * points + plane)
    square = lambda matrix: np.concatenate([two_parts(matrix)[part, :, at : at + 256] for part in range(2) for at in range(0, matrix.shape[1], 256)])
    sides = np.concatenate([two_parts(along).reshape(-1, pairs * points), two_parts(along[picks]).reshape(-1, pairs * points)], axis=1)
    blocks = [
        square(quarters),
        square(halves),
        square(odd),
        sides,
        np.pad(spread, ((0, 0), (0, 256 - spread.shape[1]))).astype(ml_dtypes.bfloat16),
    ]
    return np.concatenate(blocks)


def unpacked(ref, own, points):
    side = own * own * points
    big = [jnp.concatenate([ref[1024 + 512 * at : 1536 + 512 * at] for at in pair], axis=1) for pair in ((0, 1), (2, 3))]
    return dict(
        quarters=(ref[0:256], ref[256:512]),
        halves=(ref[512:768], ref[768:1024]),
        odd=big,
        along=ref[3072 : 3072 + 2 * side, :side],
        back=ref[3072 : 3072 + 2 * side, side : 2 * side],
        spread=ref[3072 + 2 * side : 3072 + 3 * side, : own * points],
    )


def split(value):
    high = value.astype(jnp.bfloat16)
    return high, (value - high.astype(jnp.float32)).astype(jnp.bfloat16)


def product(left, right, contract):
    return lax.dot_general(left, right, (contract, ((), ())), preferred_element_type=jnp.float32)


def on_rows(value, matrix, contract):
    rows = value.shape[0]
    high, low = split(value)
    both = product(jnp.concatenate([high, low], axis=0), matrix[0], ((1,), (contract,)))
    rest = product(high, matrix[1], ((1,), (contract,)))
    return both[:rows] + both[rows:] + rest


def on_planes(matrix, value):
    rows = matrix.shape[0] // 2
    high, low = split(value)
    both = product(matrix, high, ((1,), (0,)))
    rest = product(matrix[:rows], low, ((1,), (0,)))
    return both[:rows] + both[rows:] + rest


def in_mode_order(kernel, points):
    order = mode_order(points)
    width = 128
    each = width // points
    lane = lax.broadcasted_iota(jnp.int32, (points, width), 1)
    columns = []
    for column in range(points * points // width):
        taken = None
        for at in range(each):
            source = int(order[column * each + at])
            block = kernel[:, source // each * width : (source // each + 1) * width]
            shift = (at - source % each) * points % width
            if shift:
                block = pltpu.roll(block, shift, 1)
            taken = block if taken is None else jnp.where(lane >= at * points, block, taken)
        columns.append(taken)
    return jnp.concatenate(columns, axis=1)


def forward(mine, partner, mine_weight, partner_weight, modal, table):
    own, points, cells = mine.shape
    pairs = own * own
    block = cells // 4
    left = mine.astype(jnp.float32)
    right = partner.astype(jnp.float32)
    along = table["along"]
    parts = []
    for at in range(4):
        lanes = slice(at * block, (at + 1) * block)
        density = jnp.concatenate(
            [left[a, :, lanes] * right[b, :, lanes] for b in range(own) for a in range(own)], axis=0
        )
        parts.append(on_planes(along, density))
    even0, even1 = parts[0] + parts[2], parts[1] + parts[3]
    odd = jnp.concatenate([parts[0] - parts[2], parts[1] - parts[3]], axis=1)
    spectrum = jnp.concatenate(
        [
            on_rows(even0 + even1, table["quarters"], 0),
            on_rows(even0 - even1, table["halves"], 0),
            on_rows(odd, table["odd"], 0),
        ],
        axis=1,
    )
    energies = []
    shaped = []
    for f in range(pairs):
        rows = spectrum[f * points : (f + 1) * points]
        potential = rows * modal
        shaped.append(potential)
        terms = (rows * potential).reshape(points // 8, 8, cells // 128, 128)
        energies.append(jnp.sum(terms, axis=(0, 2)))
    energy = jnp.zeros((8, 128), jnp.float32)
    straight = jnp.zeros((8, 128), jnp.float32)
    crossed = jnp.zeros((8, 128), jnp.float32)
    for b in range(own):
        for a in range(own):
            term = energies[b * own + a] * (mine_weight[a] * partner_weight[b])
            if a == b:
                straight = straight + term
            else:
                crossed = crossed + term
    energy = straight + crossed
    return jnp.concatenate(shaped, axis=0), energy


def backward(shaped, partners, weights, table):
    own, points, cells = partners[0].shape
    block = cells // 4
    rows = own * points
    quarters = on_rows(shaped[:, :block], table["quarters"], 1)
    halves = on_rows(shaped[:, block : 2 * block], table["halves"], 1)
    odd = on_rows(shaped[:, 2 * block :], table["odd"], 1)
    even0, even1 = quarters + halves, quarters - halves
    odd0, odd1 = odd[:, :block], odd[:, block:]
    fields = [even0 + odd0, even1 + odd1, even0 - odd0, even1 - odd1]
    pulled = []
    for at in range(4):
        total = None
        for turn, (partner, weight) in enumerate(zip(partners, weights)):
            potential = on_planes(table["back"], fields[at][turn * own * rows : (turn + 1) * own * rows])
            flat = partner.reshape(own * points, cells)[:, at * block : (at + 1) * block]
            spreads = product(table["spread"], flat, ((1,), (0,)))
            for b in range(own):
                term = potential[b * rows : (b + 1) * rows] * spreads[b * rows : (b + 1) * rows] * weight[b]
                total = term if total is None else total + term
        pulled.append(-total)
    return jnp.concatenate(pulled, axis=1)


def whereabouts():
    zh, zl, core = lax.axis_index("zh"), lax.axis_index("zl"), lax.axis_index("core")
    here = lax.axis_index("y") * SIZES[2] + lax.axis_index("x")
    column = SIZES[1] * SIZES[2]
    slot = jnp.where(zh == 0, zl, SIZES[3] - 1 - zl) * SIZES[4] + core
    step = jnp.int32(0)
    for at, (dy, dx) in enumerate(pair for chip in STEPS for pair in chip):
        step = jnp.where(slot == at, dy * SIZES[2] + dx, step)
    there = jnp.bitwise_xor(here, step)
    return step, zh * column + here, zh * column + there, (1 - zh) * column + there


def prep_body(notes_ref):
    step = whereabouts()[0]
    lane = lax.broadcasted_iota(jnp.int32, (1, notes_ref.shape[1]), 1)
    notes_ref[0:1] = jnp.where(lane == step, 1.0, 0.0)
    notes_ref[1:2] = jnp.where(lane == SIZES[1] * SIZES[2] + step, 1.0, 0.0)


def picks_body(plan_ref, picks_ref):
    slots = picks_ref.shape[0]
    lane = lax.broadcasted_iota(jnp.int32, (1, picks_ref.shape[1]), 1)
    group = lax.axis_index("zl") * SIZES[4] + lax.axis_index("core")
    for slot in range(slots):
        picks_ref[slot : slot + 1] = jnp.where(lane == plan_ref[group * slots + slot], 1.0, 0.0)


def weights_of(occupation_ref, which, own):
    owner = whereabouts()[which]
    return [occupation_ref[owner * own + at] for at in range(own)]


MINE, NEAR, FAR = 1, 2, 3


def forward_body(which, *refs):
    halves = 1 if which == FAR else 2
    occupation_ref, partners = refs[0], refs[1 : 1 + halves]
    mine_ref, table_ref, kernel_ref, _, shaped_ref, energy_ref, partner_ref = refs[1 + halves :]
    own, points, _ = mine_ref.shape
    partner = partners[0][...]
    if halves == 2:
        partner = jnp.where(lax.axis_index("zh") == 0, partner, partners[1][...])
    partner_ref[...] = partner
    shaped, energy = forward(
        mine_ref[...],
        partner,
        weights_of(occupation_ref, MINE, own),
        weights_of(occupation_ref, which, own),
        in_mode_order(kernel_ref[...], points),
        unpacked(table_ref, own, points),
    )
    shaped_ref[...] = shaped
    energy_ref[...] = jnp.full(energy_ref.shape, jnp.sum(energy))


def back_body(occupation_ref, near_ref, far_ref, table_ref, near_shaped_ref, far_shaped_ref, keep_ref, send_ref):
    own, points, _ = near_ref.shape
    exchange = backward(
        jnp.concatenate([near_shaped_ref[...], far_shaped_ref[...]], axis=0),
        [near_ref[...], far_ref[...]],
        [weights_of(occupation_ref, which, own) for which in (NEAR, FAR)],
        unpacked(table_ref, own, points),
    )
    half = exchange.shape[0] // 2
    low, high = exchange[:half], exchange[half:]
    core = lax.axis_index("core")
    keep_ref[...] = jnp.where(core == 0, low, high)
    send_ref[...] = jnp.where(core == 0, high, low)


def rows_body(near_ref, across_ref, far_ref, notes_ref, out_ref):
    row = (near_ref[...] + across_ref[...]) * notes_ref[0:1] + 2.0 * far_ref[...] * notes_ref[1:2]
    out_ref[...] = jnp.broadcast_to(row[None], out_ref.shape)


def join_body(keep_ref, received_ref, energies_ref, out_ref):
    chips, each, width = out_ref.shape
    cells = keep_ref.shape[1]
    rows = energies_ref[:, 0, :]
    while rows.shape[0] > 8:
        half = rows.shape[0] // 2
        rows = rows[:half] + rows[half:]
    for shift in (4, 2, 1):
        rows = rows + pltpu.roll(rows, shift, 0)
    out_ref[:, :, :cells] = (keep_ref[...] + received_ref[...]).reshape(chips, each, cells)
    out_ref[:, :, cells:] = jnp.broadcast_to(rows[None, :each], (chips, each, width - cells))


def last_body(scale, picks_ref, pieces_ref, exchange_ref, slot_ref):
    chips, _, _ = pieces_ref.shape
    own, planes, cells = exchange_ref.shape
    total = pieces_ref[0]
    for chip in range(1, chips):
        total = total + pieces_ref[chip]
    for a in range(own):
        exchange_ref[a] = total[a * planes : (a + 1) * planes, :cells]
    levels = total[:1, cells:]
    for slot in range(slot_ref.shape[0]):
        slot_ref[slot] = jnp.sum(levels * picks_ref[slot : slot + 1]) * scale


def in_vmem(count):
    return [pl.BlockSpec(memory_space=pltpu.VMEM)] * count


def in_smem(count):
    return [pl.BlockSpec(memory_space=pltpu.SMEM)] * count


def floats(*shape):
    return jax.ShapeDtypeStruct(shape, jnp.float32)


PARAMS = pltpu.CompilerParams(vmem_limit_bytes=24 << 20)


def on_device(orbitals, kernel, occupations, plan):
    own, points, cells = orbitals.shape
    total_orbitals = occupations.shape[0]
    groups = lax.axis_size(PAIR)
    cores = lax.axis_size("core")
    chips = lax.axis_size("zl")
    slots = plan.shape[0] // groups
    column = lax.axis_size(("y", "x"))

    def moved(move, half=None):
        return lax.ppermute(orbitals, AXES, routes(move, half))

    near_low = moved(same_half, 0)
    far = moved(other_half)
    near_high = moved(same_half, 1)

    table = jnp.asarray(tables(points, own, groups, cores))
    rows = own * points
    each = rows // 2 // chips
    pairs = own * own

    def call(body, out_shape, *arrays, smem=0, smem_out=0, flops=0):
        count = len(out_shape) if isinstance(out_shape, tuple) else 0
        outs = in_vmem(max(count, 1) - smem_out) + in_smem(smem_out)
        return pl.pallas_call(
            body,
            out_shape=out_shape,
            in_specs=in_smem(smem) + in_vmem(len(arrays) - smem),
            out_specs=tuple(outs) if count else outs[0],
            cost_estimate=pl.CostEstimate(flops=flops, bytes_accessed=1 << 20, transcendentals=0),
            compiler_params=PARAMS,
        )(*arrays)

    notes = call(prep_body, floats(8, 128), flops=1 << 30)
    spectral = (floats(pairs * points, cells), floats(1, 128), jax.ShapeDtypeStruct(orbitals.shape, orbitals.dtype))
    work = 6 * pairs * points * cells * (pairs * points + 384)
    shared = (orbitals, table, kernel, notes)
    near_shaped, near_energy, near = call(
        functools.partial(forward_body, NEAR), spectral, occupations, near_low, near_high, *shared, smem=1, flops=work
    )
    across = lax.ppermute(near_energy, AXES, routes(mirror))
    picks = call(picks_body, floats(slots, 128), plan, smem=1)
    far_shaped, far_energy, far = call(
        functools.partial(forward_body, FAR), spectral, occupations, far, *shared, smem=1, flops=work
    )
    energies = call(rows_body, floats(column * cores, 1, 128), near_energy, across, far_energy, notes)
    everyone = lax.all_to_all(energies, ("y", "x", "core"), 0, 0, tiled=True)
    half = floats(rows // 2, cells)
    keep, send = call(
        back_body, (half, half), occupations, near, far, table, near_shaped, far_shaped, smem=1, flops=2 * work
    )
    received = lax.ppermute(send, AXES, routes(other_core))
    joined = call(join_body, floats(chips, each, cells + 128), keep, received, everyone)
    pieces = lax.all_to_all(joined, "zl", 0, 0, tiled=True)
    scale = -1.0 / (2.0 * total_orbitals * points**3)
    outs = (floats(own, each // own, cells), floats(slots))
    return call(functools.partial(last_body, scale), outs, picks, pieces, smem_out=1)


def solution(mesh):
    split_mesh = Mesh(mesh.devices.reshape(SIZES), AXES)

    return jax.shard_map(
        on_device,
        mesh=split_mesh,
        in_specs=(P(BAND, None, None), P(), P(), P()),
        out_specs=(P(BAND, PAIR, None), P(PAIR)),
        check_vma=False,
    )
```

```python
import functools
import math

import jax
import jax.numpy as jnp
import ml_dtypes
import numpy as np
from jax import lax
from jax.experimental import pallas as pl
from jax.experimental.pallas import tpu as pltpu
from jax.sharding import Mesh
from jax.sharding import PartitionSpec as P

AXES = ("zh", "y", "x", "zl", "core")
BAND = ("zh", "y", "x")
PAIR = ("zl", "core")
SIZES = (2, 4, 4, 8, 2)

STEPS = (
    ((2, 2), (2, 1)),
    ((2, 3), (3, 2)),
    ((3, 3), (3, 1)),
    ((0, 0), (1, 0)),
    ((0, 1), (0, 3)),
    ((1, 3), (1, 1)),
    ((0, 2), (3, 0)),
    ((1, 2), (2, 0)),
)


def step_of(zh, zl, core):
    return STEPS[zl if zh == 0 else SIZES[3] - 1 - zl][core]


def place(coords):
    flat = 0
    for size, at in zip(SIZES, coords):
        flat = flat * size + at
    return flat


def routes(move, half=None):
    return [(place(c), place(move(*c))) for c in np.ndindex(*SIZES) if half in (None, c[0])]


def same_half(zh, y, x, zl, core):
    dy, dx = step_of(zh, zl, core)
    return zh, y ^ dy, x ^ dx, zl, core


def other_half(zh, y, x, zl, core):
    dy, dx = step_of(zh, zl, core)
    return 1 - zh, y ^ dy, x ^ dx, SIZES[3] - 1 - zl, core


def mirror(zh, y, x, zl, core):
    return 1 - zh, y, x, SIZES[3] - 1 - zl, core


def other_core(zh, y, x, zl, core):
    return zh, y, x, zl, 1 - core


def two_parts(matrix):
    high = matrix.astype(ml_dtypes.bfloat16)
    low = (matrix - high.astype(np.float64)).astype(ml_dtypes.bfloat16)
    return np.stack([high, low])


def hartley(points):
    at = np.arange(points)
    angle = (np.outer(at, at) % points) * (2.0 * math.pi / points)
    return (np.cos(angle) + np.sin(angle)) / math.sqrt(points)


def mode_order(points):
    at = np.arange(points)
    return np.concatenate([at[0::4], at[2::4], at[1::2]])


@functools.cache
def tables(points, own, groups, cores):
    base = hartley(points)
    quarter = base[:, : points // 4]
    quarters = np.kron(quarter[0::4].T, base)
    halves = np.kron(quarter[2::4].T, base)
    odd = np.kron(base[1::2, : points // 2].T, base)
    pairs = own * own
    along = np.kron(np.eye(pairs), base)
    planes = points // groups
    rows = []
    for core in range(cores):
        for zl in range(groups // cores):
            for a in range(own):
                for low in range(planes):
                    rows.append((a, (zl * cores + core) * planes + low))
    picks = []
    spread = np.zeros((pairs * points, own * points))
    for b in range(own):
        for a, plane in rows:
            spread[len(picks), b * points + plane] = 1.0
            picks.append((b * own + a) * points + plane)
    square = lambda matrix: np.concatenate([two_parts(matrix)[part, :, at : at + 256] for part in range(2) for at in range(0, matrix.shape[1], 256)])
    sides = np.concatenate([two_parts(along).reshape(-1, pairs * points), two_parts(along[picks]).reshape(-1, pairs * points)], axis=1)
    blocks = [
        square(quarters),
        square(halves),
        square(odd),
        sides,
        np.pad(spread, ((0, 0), (0, 256 - spread.shape[1]))).astype(ml_dtypes.bfloat16),
    ]
    return np.concatenate(blocks)


def unpacked(ref, own, points):
    side = own * own * points
    big = [jnp.concatenate([ref[1024 + 512 * at : 1536 + 512 * at] for at in pair], axis=1) for pair in ((0, 1), (2, 3))]
    return dict(
        quarters=(ref[0:256], ref[256:512]),
        halves=(ref[512:768], ref[768:1024]),
        odd=big,
        along=ref[3072 : 3072 + 2 * side, :side],
        back=ref[3072 : 3072 + 2 * side, side : 2 * side],
        spread=ref[3072 + 2 * side : 3072 + 3 * side, : own * points],
    )


def split(value):
    high = value.astype(jnp.bfloat16)
    return high, (value - high.astype(jnp.float32)).astype(jnp.bfloat16)


def product(left, right, contract):
    return lax.dot_general(left, right, (contract, ((), ())), preferred_element_type=jnp.float32)


def on_rows(value, matrix, contract):
    rows = value.shape[0]
    high, low = split(value)
    both = product(jnp.concatenate([high, low], axis=0), matrix[0], ((1,), (contract,)))
    rest = product(high, matrix[1], ((1,), (contract,)))
    return both[:rows] + both[rows:] + rest


def on_planes(matrix, value):
    rows = matrix.shape[0] // 2
    high, low = split(value)
    both = product(matrix, high, ((1,), (0,)))
    rest = product(matrix[:rows], low, ((1,), (0,)))
    return both[:rows] + both[rows:] + rest


def in_mode_order(kernel, points):
    order = mode_order(points)
    width = 128
    each = width // points
    lane = lax.broadcasted_iota(jnp.int32, (points, width), 1)
    columns = []
    for column in range(points * points // width):
        taken = None
        for at in range(each):
            source = int(order[column * each + at])
            block = kernel[:, source // each * width : (source // each + 1) * width]
            shift = (at - source % each) * points % width
            if shift:
                block = pltpu.roll(block, shift, 1)
            taken = block if taken is None else jnp.where(lane >= at * points, block, taken)
        columns.append(taken)
    return jnp.concatenate(columns, axis=1)


def forward(mine, partner, mine_weight, partner_weight, modal, table):
    own, points, cells = mine.shape
    pairs = own * own
    block = cells // 4
    left = mine.astype(jnp.float32)
    right = partner.astype(jnp.float32)
    along = table["along"]
    parts = []
    for at in range(4):
        lanes = slice(at * block, (at + 1) * block)
        density = jnp.concatenate(
            [left[a, :, lanes] * right[b, :, lanes] for b in range(own) for a in range(own)], axis=0
        )
        parts.append(on_planes(along, density))
    even0, even1 = parts[0] + parts[2], parts[1] + parts[3]
    odd = jnp.concatenate([parts[0] - parts[2], parts[1] - parts[3]], axis=1)
    spectrum = jnp.concatenate(
        [
            on_rows(even0 + even1, table["quarters"], 0),
            on_rows(even0 - even1, table["halves"], 0),
            on_rows(odd, table["odd"], 0),
        ],
        axis=1,
    )
    energies = []
    shaped = []
    for f in range(pairs):
        rows = spectrum[f * points : (f + 1) * points]
        potential = rows * modal
        shaped.append(potential)
        terms = (rows * potential).reshape(points // 8, 8, cells // 128, 128)
        energies.append(jnp.sum(terms, axis=(0, 2)))
    energy = jnp.zeros((8, 128), jnp.float32)
    straight = jnp.zeros((8, 128), jnp.float32)
    crossed = jnp.zeros((8, 128), jnp.float32)
    for b in range(own):
        for a in range(own):
            term = energies[b * own + a] * (mine_weight[a] * partner_weight[b])
            if a == b:
                straight = straight + term
            else:
                crossed = crossed + term
    energy = straight + crossed
    return jnp.concatenate(shaped, axis=0), energy


def backward(shaped, partners, weights, table):
    own, points, cells = partners[0].shape
    block = cells // 4
    rows = own * points
    quarters = on_rows(shaped[:, :block], table["quarters"], 1)
    halves = on_rows(shaped[:, block : 2 * block], table["halves"], 1)
    odd = on_rows(shaped[:, 2 * block :], table["odd"], 1)
    even0, even1 = quarters + halves, quarters - halves
    odd0, odd1 = odd[:, :block], odd[:, block:]
    fields = [even0 + odd0, even1 + odd1, even0 - odd0, even1 - odd1]
    pulled = []
    for at in range(4):
        total = None
        for turn, (partner, weight) in enumerate(zip(partners, weights)):
            potential = on_planes(table["back"], fields[at][turn * own * rows : (turn + 1) * own * rows])
            flat = partner.reshape(own * points, cells)[:, at * block : (at + 1) * block]
            spreads = product(table["spread"], flat, ((1,), (0,)))
            for b in range(own):
                term = potential[b * rows : (b + 1) * rows] * spreads[b * rows : (b + 1) * rows] * weight[b]
                total = term if total is None else total + term
        pulled.append(-total)
    return jnp.concatenate(pulled, axis=1)


def whereabouts():
    zh, zl, core = lax.axis_index("zh"), lax.axis_index("zl"), lax.axis_index("core")
    here = lax.axis_index("y") * SIZES[2] + lax.axis_index("x")
    column = SIZES[1] * SIZES[2]
    slot = jnp.where(zh == 0, zl, SIZES[3] - 1 - zl) * SIZES[4] + core
    step = jnp.int32(0)
    for at, (dy, dx) in enumerate(pair for chip in STEPS for pair in chip):
        step = jnp.where(slot == at, dy * SIZES[2] + dx, step)
    there = jnp.bitwise_xor(here, step)
    return step, zh * column + here, zh * column + there, (1 - zh) * column + there


def prep_body(occupation_ref, notes_ref):
    step, *owners = whereabouts()
    lane = lax.broadcasted_iota(jnp.int32, (1, notes_ref.shape[1]), 1)
    rows = [jnp.full(lane.shape, occupation_ref[owner * 2 + at]) for owner in owners for at in range(2)]
    rows += [jnp.where(lane == level, 1.0, 0.0) for level in (step, SIZES[1] * SIZES[2] + step)]
    for at, row in enumerate(rows):
        notes_ref[at : at + 1] = row


def picks_body(plan_ref, picks_ref):
    slots = picks_ref.shape[0]
    lane = lax.broadcasted_iota(jnp.int32, (1, picks_ref.shape[1]), 1)
    group = lax.axis_index("zl") * SIZES[4] + lax.axis_index("core")
    for slot in range(slots):
        picks_ref[slot : slot + 1] = jnp.where(lane == plan_ref[group * slots + slot], 1.0, 0.0)


def mine_of(low_ref, high_ref):
    return jnp.where(lax.axis_index("zh") == 0, low_ref[...], high_ref[...])


def weights_of(notes_ref, which, own):
    return [notes_ref[which * own + at : which * own + at + 1, 0:1] for at in range(own)]


NEAR, FAR = 1, 2


def forward_body(which, half, partner_ref, mine_ref, table_ref, kernel_ref, notes_ref, shaped_ref, energy_ref):
    own, points, _ = mine_ref.shape

    def run():
        shaped, energy = forward(
            mine_ref[...],
            partner_ref[...],
            weights_of(notes_ref, 0, own),
            weights_of(notes_ref, which, own),
            in_mode_order(kernel_ref[...], points),
            unpacked(table_ref, own, points),
        )
        shaped_ref[...] = shaped
        energy_ref[...] = jnp.full(energy_ref.shape, jnp.sum(energy))

    if half is None:
        run()
    else:
        pl.when(lax.axis_index("zh") == half)(run)


def back_body(low_ref, high_ref, far_ref, table_ref, notes_ref, low_shaped_ref, high_shaped_ref, far_shaped_ref, keep_ref, send_ref):
    own, points, _ = far_ref.shape
    exchange = backward(
        jnp.concatenate([mine_of(low_shaped_ref, high_shaped_ref), far_shaped_ref[...]], axis=0),
        [mine_of(low_ref, high_ref), far_ref[...]],
        [weights_of(notes_ref, which, own) for which in (NEAR, FAR)],
        unpacked(table_ref, own, points),
    )
    half = exchange.shape[0] // 2
    low, high = exchange[:half], exchange[half:]
    core = lax.axis_index("core")
    keep_ref[...] = jnp.where(core == 0, low, high)
    send_ref[...] = jnp.where(core == 0, high, low)


def rows_body(low_ref, high_ref, down_ref, up_ref, far_ref, notes_ref, out_ref):
    near = mine_of(low_ref, high_ref) + mine_of(down_ref, up_ref)
    row = near * notes_ref[6:7] + 2.0 * far_ref[...] * notes_ref[7:8]
    out_ref[...] = jnp.broadcast_to(row[None], out_ref.shape)


def join_body(keep_ref, received_ref, energies_ref, out_ref):
    chips, each, width = out_ref.shape
    cells = keep_ref.shape[1]
    rows = energies_ref[:, 0, :]
    while rows.shape[0] > 8:
        half = rows.shape[0] // 2
        rows = rows[:half] + rows[half:]
    for shift in (4, 2, 1):
        rows = rows + pltpu.roll(rows, shift, 0)
    out_ref[:, :, :cells] = (keep_ref[...] + received_ref[...]).reshape(chips, each, cells)
    out_ref[:, :, cells:] = jnp.broadcast_to(rows[None, :each], (chips, each, width - cells))


def last_body(scale, picks_ref, pieces_ref, exchange_ref, slot_ref):
    chips, _, _ = pieces_ref.shape
    own, planes, cells = exchange_ref.shape
    total = pieces_ref[0]
    for chip in range(1, chips):
        total = total + pieces_ref[chip]
    for a in range(own):
        exchange_ref[a] = total[a * planes : (a + 1) * planes, :cells]
    levels = total[:1, cells:]
    for slot in range(slot_ref.shape[0]):
        slot_ref[slot] = jnp.sum(levels * picks_ref[slot : slot + 1]) * scale


def in_vmem(count):
    return [pl.BlockSpec(memory_space=pltpu.VMEM)] * count


def in_smem(count):
    return [pl.BlockSpec(memory_space=pltpu.SMEM)] * count


def floats(*shape):
    return jax.ShapeDtypeStruct(shape, jnp.float32)


PARAMS = pltpu.CompilerParams(vmem_limit_bytes=24 << 20)


def on_device(orbitals, kernel, occupations, plan):
    own, points, cells = orbitals.shape
    total_orbitals = occupations.shape[0]
    groups = lax.axis_size(PAIR)
    cores = lax.axis_size("core")
    chips = lax.axis_size("zl")
    slots = plan.shape[0] // groups
    column = lax.axis_size(("y", "x"))

    def moved(value, move, half=None):
        return lax.ppermute(value, AXES, routes(move, half))

    near_low = moved(orbitals, same_half, 0)
    far = moved(orbitals, other_half)
    near_high = moved(orbitals, same_half, 1)

    table = jnp.asarray(tables(points, own, groups, cores))
    rows = own * points
    each = rows // 2 // chips
    pairs = own * own

    def call(body, out_shape, *arrays, smem=0, smem_out=0, flops=0):
        count = len(out_shape) if isinstance(out_shape, tuple) else 0
        outs = in_vmem(max(count, 1) - smem_out) + in_smem(smem_out)
        return pl.pallas_call(
            body,
            out_shape=out_shape,
            in_specs=in_smem(smem) + in_vmem(len(arrays) - smem),
            out_specs=tuple(outs) if count else outs[0],
            cost_estimate=pl.CostEstimate(flops=flops, bytes_accessed=1 << 20, transcendentals=0),
            compiler_params=PARAMS,
        )(*arrays)

    notes = call(prep_body, floats(8, 128), occupations, smem=1, flops=1 << 30)
    spectral = (floats(pairs * points, cells), floats(1, 128))
    work = 6 * pairs * points * cells * (pairs * points + 384)
    shared = (orbitals, table, kernel, notes)

    def forwards(which, half, partner):
        body = functools.partial(forward_body, which, half)
        return call(body, spectral, partner, *shared, flops=work)

    low_shaped, low_energy = forwards(NEAR, 0, near_low)
    up = moved(low_energy, mirror, 0)
    high_shaped, high_energy = forwards(NEAR, 1, near_high)
    down = moved(high_energy, mirror, 1)
    picks = call(picks_body, floats(slots, 128), plan, smem=1)
    far_shaped, far_energy = forwards(FAR, None, far)
    energies = call(rows_body, floats(column * cores, 1, 128), low_energy, high_energy, down, up, far_energy, notes)
    everyone = lax.all_to_all(energies, ("y", "x", "core"), 0, 0, tiled=True)
    half = floats(rows // 2, cells)
    shaped = (low_shaped, high_shaped, far_shaped)
    keep, send = call(back_body, (half, half), near_low, near_high, far, table, notes, *shaped, flops=2 * work)
    received = lax.ppermute(send, AXES, routes(other_core))
    joined = call(join_body, floats(chips, each, cells + 128), keep, received, everyone)
    pieces = lax.all_to_all(joined, "zl", 0, 0, tiled=True)
    scale = -1.0 / (2.0 * total_orbitals * points**3)
    outs = (floats(own, each // own, cells), floats(slots))
    return call(functools.partial(last_body, scale), outs, picks, pieces, smem_out=1)


def solution(mesh):
    split_mesh = Mesh(mesh.devices.reshape(SIZES), AXES)

    return jax.shard_map(
        on_device,
        mesh=split_mesh,
        in_specs=(P(BAND, None, None), P(), P(), P()),
        out_specs=(P(BAND, PAIR, None), P(PAIR)),
        check_vma=False,
    )
```

```python
import functools
import math

import jax
import jax.numpy as jnp
import ml_dtypes
import numpy as np
from jax import lax
from jax.experimental import pallas as pl
from jax.experimental.pallas import tpu as pltpu
from jax.sharding import Mesh
from jax.sharding import PartitionSpec as P

AXES = ("zh", "y", "x", "zl", "core")
BAND = ("zh", "y", "x")
PAIR = ("zl", "core")
SIZES = (2, 4, 4, 8, 2)

STEPS = (
    ((2, 2), (2, 1)),
    ((2, 3), (3, 2)),
    ((3, 3), (3, 1)),
    ((0, 0), (1, 0)),
    ((0, 1), (0, 3)),
    ((1, 3), (3, 0)),
    ((0, 2), (1, 1)),
    ((1, 2), (2, 0)),
)


def step_of(zh, zl, core):
    return STEPS[zl if zh == 0 else SIZES[3] - 1 - zl][core]


def place(coords):
    flat = 0
    for size, at in zip(SIZES, coords):
        flat = flat * size + at
    return flat


def routes(move):
    return [(place(c), place(move(*c))) for c in np.ndindex(*SIZES)]


def same_half(zh, y, x, zl, core):
    dy, dx = step_of(zh, zl, core)
    return zh, y ^ dy, x ^ dx, zl, core


def other_half(zh, y, x, zl, core):
    dy, dx = step_of(zh, zl, core)
    return 1 - zh, y ^ dy, x ^ dx, SIZES[3] - 1 - zl, core


def mirror(zh, y, x, zl, core):
    return 1 - zh, y, x, SIZES[3] - 1 - zl, core


def other_core(zh, y, x, zl, core):
    return zh, y, x, zl, 1 - core


def two_parts(matrix):
    high = matrix.astype(ml_dtypes.bfloat16)
    low = (matrix - high.astype(np.float64)).astype(ml_dtypes.bfloat16)
    return np.stack([high, low])


def hartley(points):
    at = np.arange(points)
    angle = (np.outer(at, at) % points) * (2.0 * math.pi / points)
    return (np.cos(angle) + np.sin(angle)) / math.sqrt(points)


def mode_order(points):
    at = np.arange(points)
    return np.concatenate([at[0::4], at[2::4], at[1::2]])


@functools.cache
def tables(points, own, groups, cores):
    base = hartley(points)
    quarter = base[:, : points // 4]
    quarters = np.kron(quarter[0::4].T, base)
    halves = np.kron(quarter[2::4].T, base)
    odd = np.kron(base[1::2, : points // 2].T, base)
    pairs = own * own
    along = np.kron(np.eye(pairs), base)
    planes = points // groups
    rows = []
    for core in range(cores):
        for zl in range(groups // cores):
            for a in range(own):
                for low in range(planes):
                    rows.append((a, (zl * cores + core) * planes + low))
    picks = []
    spread = np.zeros((pairs * points, own * points))
    for b in range(own):
        for a, plane in rows:
            spread[len(picks), b * points + plane] = 1.0
            picks.append((b * own + a) * points + plane)
    square = lambda matrix: np.concatenate([two_parts(matrix)[part, :, at : at + 256] for part in range(2) for at in range(0, matrix.shape[1], 256)])
    sides = np.concatenate([two_parts(along).reshape(-1, pairs * points), two_parts(along[picks]).reshape(-1, pairs * points)], axis=1)
    blocks = [
        square(quarters),
        square(halves),
        square(odd),
        sides,
        np.pad(spread, ((0, 0), (0, 256 - spread.shape[1]))).astype(ml_dtypes.bfloat16),
    ]
    return np.concatenate(blocks)


def unpacked(ref, own, points):
    side = own * own * points
    big = [jnp.concatenate([ref[1024 + 512 * at : 1536 + 512 * at] for at in pair], axis=1) for pair in ((0, 1), (2, 3))]
    return dict(
        quarters=(ref[0:256], ref[256:512]),
        halves=(ref[512:768], ref[768:1024]),
        odd=big,
        along=ref[3072 : 3072 + 2 * side, :side],
        back=ref[3072 : 3072 + 2 * side, side : 2 * side],
        spread=ref[3072 + 2 * side : 3072 + 3 * side, : own * points],
    )


def split(value):
    high = value.astype(jnp.bfloat16)
    return high, (value - high.astype(jnp.float32)).astype(jnp.bfloat16)


def product(left, right, contract):
    return lax.dot_general(left, right, (contract, ((), ())), preferred_element_type=jnp.float32)


def on_rows(value, matrix, contract):
    rows = value.shape[0]
    high, low = split(value)
    both = product(jnp.concatenate([high, low], axis=0), matrix[0], ((1,), (contract,)))
    rest = product(high, matrix[1], ((1,), (contract,)))
    return both[:rows] + both[rows:] + rest


def on_planes(matrix, value):
    rows = matrix.shape[0] // 2
    high, low = split(value)
    both = product(matrix, high, ((1,), (0,)))
    rest = product(matrix[:rows], low, ((1,), (0,)))
    return both[:rows] + both[rows:] + rest


def in_mode_order(kernel, points):
    order = mode_order(points)
    width = 128
    each = width // points
    lane = lax.broadcasted_iota(jnp.int32, (points, width), 1)
    columns = []
    for column in range(points * points // width):
        taken = None
        for at in range(each):
            source = int(order[column * each + at])
            block = kernel[:, source // each * width : (source // each + 1) * width]
            shift = (at - source % each) * points % width
            if shift:
                block = pltpu.roll(block, shift, 1)
            taken = block if taken is None else jnp.where(lane >= at * points, block, taken)
        columns.append(taken)
    return jnp.concatenate(columns, axis=1)


def forward(mine, partner, mine_weight, partner_weight, modal, table):
    own, points, cells = mine.shape
    pairs = own * own
    block = cells // 4
    left = mine.astype(jnp.float32)
    right = partner.astype(jnp.float32)
    along = table["along"]
    parts = []
    for at in range(4):
        lanes = slice(at * block, (at + 1) * block)
        density = jnp.concatenate(
            [left[a, :, lanes] * right[b, :, lanes] for b in range(own) for a in range(own)], axis=0
        )
        parts.append(on_planes(along, density))
    even0, even1 = parts[0] + parts[2], parts[1] + parts[3]
    odd = jnp.concatenate([parts[0] - parts[2], parts[1] - parts[3]], axis=1)
    spectrum = jnp.concatenate(
        [
            on_rows(even0 + even1, table["quarters"], 0),
            on_rows(even0 - even1, table["halves"], 0),
            on_rows(odd, table["odd"], 0),
        ],
        axis=1,
    )
    energies = []
    shaped = []
    for f in range(pairs):
        rows = spectrum[f * points : (f + 1) * points]
        potential = rows * modal
        shaped.append(potential)
        terms = (rows * potential).reshape(points // 8, 8, cells // 128, 128)
        energies.append(jnp.sum(terms, axis=(0, 2)))
    energy = jnp.zeros((8, 128), jnp.float32)
    straight = jnp.zeros((8, 128), jnp.float32)
    crossed = jnp.zeros((8, 128), jnp.float32)
    for b in range(own):
        for a in range(own):
            term = energies[b * own + a] * (mine_weight[a] * partner_weight[b])
            if a == b:
                straight = straight + term
            else:
                crossed = crossed + term
    energy = straight + crossed
    return jnp.concatenate(shaped, axis=0), energy


def backward(shaped, partners, weights, table):
    own, points, cells = partners[0].shape
    block = cells // 4
    rows = own * points
    quarters = on_rows(shaped[:, :block], table["quarters"], 1)
    halves = on_rows(shaped[:, block : 2 * block], table["halves"], 1)
    odd = on_rows(shaped[:, 2 * block :], table["odd"], 1)
    even0, even1 = quarters + halves, quarters - halves
    odd0, odd1 = odd[:, :block], odd[:, block:]
    fields = [even0 + odd0, even1 + odd1, even0 - odd0, even1 - odd1]
    pulled = []
    for at in range(4):
        total = None
        for turn, (partner, weight) in enumerate(zip(partners, weights)):
            potential = on_planes(table["back"], fields[at][turn * own * rows : (turn + 1) * own * rows])
            flat = partner.reshape(own * points, cells)[:, at * block : (at + 1) * block]
            spreads = product(table["spread"], flat, ((1,), (0,)))
            for b in range(own):
                term = potential[b * rows : (b + 1) * rows] * spreads[b * rows : (b + 1) * rows] * weight[b]
                total = term if total is None else total + term
        pulled.append(-total)
    return jnp.concatenate(pulled, axis=1)


def whereabouts():
    zh, zl, core = lax.axis_index("zh"), lax.axis_index("zl"), lax.axis_index("core")
    here = lax.axis_index("y") * SIZES[2] + lax.axis_index("x")
    column = SIZES[1] * SIZES[2]
    slot = jnp.where(zh == 0, zl, SIZES[3] - 1 - zl) * SIZES[4] + core
    step = jnp.int32(0)
    for at, (dy, dx) in enumerate(pair for chip in STEPS for pair in chip):
        step = jnp.where(slot == at, dy * SIZES[2] + dx, step)
    there = jnp.bitwise_xor(here, step)
    return step, zh * column + here, zh * column + there, (1 - zh) * column + there


def masks_body(masks_ref):
    step = whereabouts()[0]
    lane = lax.broadcasted_iota(jnp.int32, (1, masks_ref.shape[1]), 1)
    masks_ref[0:1] = jnp.where(lane == step, 1.0, 0.0)
    masks_ref[1:2] = jnp.where(lane == SIZES[1] * SIZES[2] + step, 1.0, 0.0)


def prep_body(occupation_ref, masks_ref, notes_ref):
    _, *owners = whereabouts()
    lane = lax.broadcasted_iota(jnp.int32, (1, notes_ref.shape[1]), 1)
    rows = [jnp.full(lane.shape, occupation_ref[owner * 2 + at]) for owner in owners for at in range(2)]
    for at, row in enumerate(rows):
        notes_ref[at : at + 1] = row
    notes_ref[len(rows) : len(rows) + 2] = masks_ref[...]


def picks_body(plan_ref, picks_ref):
    slots = picks_ref.shape[0]
    lane = lax.broadcasted_iota(jnp.int32, (1, picks_ref.shape[1]), 1)
    group = lax.axis_index("zl") * SIZES[4] + lax.axis_index("core")
    for slot in range(slots):
        picks_ref[slot : slot + 1] = jnp.where(lane == plan_ref[group * slots + slot], 1.0, 0.0)


def weights_of(notes_ref, which, own):
    return [notes_ref[which * own + at : which * own + at + 1, 0:1] for at in range(own)]


NEAR, FAR = 1, 2


def forward_body(which, partner_ref, mine_ref, table_ref, kernel_ref, notes_ref, shaped_ref, energy_ref):
    own, points, _ = mine_ref.shape
    shaped, energy = forward(
        mine_ref[...],
        partner_ref[...],
        weights_of(notes_ref, 0, own),
        weights_of(notes_ref, which, own),
        in_mode_order(kernel_ref[...], points),
        unpacked(table_ref, own, points),
    )
    shaped_ref[...] = shaped
    energy_ref[...] = jnp.full(energy_ref.shape, jnp.sum(energy))


def back_body(near_ref, far_ref, table_ref, notes_ref, near_shaped_ref, far_shaped_ref, keep_ref, send_ref):
    own, points, _ = near_ref.shape
    exchange = backward(
        jnp.concatenate([near_shaped_ref[...], far_shaped_ref[...]], axis=0),
        [near_ref[...], far_ref[...]],
        [weights_of(notes_ref, which, own) for which in (NEAR, FAR)],
        unpacked(table_ref, own, points),
    )
    half = exchange.shape[0] // 2
    low, high = exchange[:half], exchange[half:]
    core = lax.axis_index("core")
    keep_ref[...] = jnp.where(core == 0, low, high)
    send_ref[...] = jnp.where(core == 0, high, low)


def rows_body(near_ref, across_ref, far_ref, notes_ref, out_ref):
    row = (near_ref[...] + across_ref[...]) * notes_ref[6:7] + 2.0 * far_ref[...] * notes_ref[7:8]
    out_ref[...] = jnp.broadcast_to(row[None], out_ref.shape)


def join_body(keep_ref, received_ref, energies_ref, out_ref):
    chips, each, width = out_ref.shape
    cells = keep_ref.shape[1]
    rows = energies_ref[:, 0, :]
    while rows.shape[0] > 8:
        half = rows.shape[0] // 2
        rows = rows[:half] + rows[half:]
    for shift in (4, 2, 1):
        rows = rows + pltpu.roll(rows, shift, 0)
    out_ref[:, :, :cells] = (keep_ref[...] + received_ref[...]).reshape(chips, each, cells)
    out_ref[:, :, cells:] = jnp.broadcast_to(rows[None, :each], (chips, each, width - cells))


def last_body(scale, picks_ref, pieces_ref, exchange_ref, slot_ref):
    chips, _, _ = pieces_ref.shape
    own, planes, cells = exchange_ref.shape
    total = pieces_ref[0]
    for chip in range(1, chips):
        total = total + pieces_ref[chip]
    for a in range(own):
        exchange_ref[a] = total[a * planes : (a + 1) * planes, :cells]
    levels = total[:1, cells:]
    for slot in range(slot_ref.shape[0]):
        slot_ref[slot] = jnp.sum(levels * picks_ref[slot : slot + 1]) * scale


def in_vmem(count):
    return [pl.BlockSpec(memory_space=pltpu.VMEM)] * count


def in_smem(count):
    return [pl.BlockSpec(memory_space=pltpu.SMEM)] * count


def floats(*shape):
    return jax.ShapeDtypeStruct(shape, jnp.float32)


PARAMS = pltpu.CompilerParams(vmem_limit_bytes=24 << 20)


def on_device(orbitals, kernel, occupations, plan):
    own, points, cells = orbitals.shape
    total_orbitals = occupations.shape[0]
    groups = lax.axis_size(PAIR)
    cores = lax.axis_size("core")
    chips = lax.axis_size("zl")
    slots = plan.shape[0] // groups
    column = lax.axis_size(("y", "x"))

    near = lax.ppermute(orbitals, AXES, routes(same_half))
    far = lax.ppermute(orbitals, AXES, routes(other_half))

    table = jnp.asarray(tables(points, own, groups, cores))
    rows = own * points
    each = rows // 2 // chips
    pairs = own * own

    def call(body, out_shape, *arrays, smem=0, smem_out=0, flops=0):
        count = len(out_shape) if isinstance(out_shape, tuple) else 0
        outs = in_vmem(max(count, 1) - smem_out) + in_smem(smem_out)
        return pl.pallas_call(
            body,
            out_shape=out_shape,
            in_specs=in_smem(smem) + in_vmem(len(arrays) - smem),
            out_specs=tuple(outs) if count else outs[0],
            cost_estimate=pl.CostEstimate(flops=flops, bytes_accessed=1 << 20, transcendentals=0),
            compiler_params=PARAMS,
        )(*arrays)

    masks = call(masks_body, floats(2, 128), flops=1 << 30)
    notes = call(prep_body, floats(8, 128), occupations, masks, smem=1)
    spectral = (floats(pairs * points, cells), floats(1, 128))
    work = 6 * pairs * points * cells * (pairs * points + 384)
    near_shaped, near_energy = call(
        functools.partial(forward_body, NEAR), spectral, near, orbitals, table, kernel, notes, flops=work
    )
    across = lax.ppermute(near_energy, AXES, routes(mirror))
    far_shaped, far_energy = call(
        functools.partial(forward_body, FAR), spectral, far, orbitals, table, kernel, notes, flops=work
    )
    energies = call(rows_body, floats(column * cores, 1, 128), near_energy, across, far_energy, notes)
    everyone = lax.all_to_all(energies, ("y", "x", "core"), 0, 0, tiled=True)
    half = floats(rows // 2, cells)
    keep, send = call(back_body, (half, half), near, far, table, notes, near_shaped, far_shaped, flops=2 * work)
    picks = call(picks_body, floats(slots, 128), plan, smem=1)
    received = lax.ppermute(send, AXES, routes(other_core))
    joined = call(join_body, floats(chips, each, cells + 128), keep, received, everyone)
    pieces = lax.all_to_all(joined, "zl", 0, 0, tiled=True)
    scale = -1.0 / (2.0 * total_orbitals * points**3)
    outs = (floats(own, each // own, cells), floats(slots))
    return call(functools.partial(last_body, scale), outs, picks, pieces, smem_out=1)


def solution(mesh):
    split_mesh = Mesh(mesh.devices.reshape(SIZES), AXES)

    return jax.shard_map(
        on_device,
        mesh=split_mesh,
        in_specs=(P(BAND, None, None), P(), P(), P()),
        out_specs=(P(BAND, PAIR, None), P(PAIR)),
        check_vma=False,
    )
```
